32 devices in a mesh: ctx: 16 (over z, y, core), req: 2 (over x).
Axes of the slice: x: 2, y: 2, z: 4, core: 2. Of those that a mesh axis runs over, the one named last changes fastest.
Arguments:
- hidden: bfloat16 [256, 5120], P('req'), parts along dimension 0, may hold values from -6 to 6
- w_query: bfloat16 [5120, 8192], P(None, 'ctx'), may hold values from -0.078125 to 0.078125
- key_projection_weight: bfloat16 [5120, 1024], P(None, 'ctx'), may hold values from -0.078125 to 0.078125
- value_projection_weight: bfloat16 [5120, 1024], P(None, 'ctx'), may hold values from -0.078125 to 0.078125
- query_gain: float32 [128], replicated, may hold values from 0.5 to 1.5
- key_gain: float32 [128], replicated, may hold values from 4 to 8
- stored_cache_keys: bfloat16 [4096, 1024], P(('req', 'ctx')), parts along dimension 0, may hold values from -100 to 100
- stored_cache_values: bfloat16 [4096, 1024], P(('req', 'ctx')), parts along dimension 0, may hold values from -8 to 8
- cache_length: int32 [2], P('req'), parts along dimension 0, may hold values from 1024 to 2048
- first_position: int32 [2], P('req'), parts along dimension 0, may hold values from 0 to 4095
Outputs:
- attended: bfloat16 [256, 8192], P('req', 'ctx'), parts along dimension 0
The draws below stay inside these ranges and needn't reach their ends.
There are 2 independent parts, one for each index of `req`. The reference program is written for one: setup_inputs(seed, part) draws one part's arguments, and reference() takes and returns one part's arrays. A program takes and returns all parts, laid end to end along the dimension named above; an argument that names none is the same for every part. Nothing has to cross between parts.
All inputs are finite; a program needn't handle non-finite values.
Results may differ from the reference program's by a relative error of at most 0.013.
The reference program's roundings to bfloat16 on the way count: a program that leaves them out, or rounds other values in their place, can miss the bound.
Values may be sent and summed in bfloat16 or wider, within the bound.
A program may use at most 128 MiB of HBM per device.

```python
import math
import jax
import jax.numpy as jnp
from jax import lax

MODEL_WIDTH = 5120
QUERY_HEADS = 64
KEY_VALUE_HEADS = 8
HEAD_SIZE = 128
NEW = 128
CACHE_SLOTS = 2048


def draw_stored_cache_keys(key, part):
    rotary_base = jax.random.normal(jax.random.fold_in(key, 11), (CACHE_SLOTS, KEY_VALUE_HEADS * HEAD_SIZE), jnp.float32) * 2.5
    return jnp.clip(rotary_base, -100.0, 100.0).astype(jnp.bfloat16)


def level_of(stream_key, extent, shards, low, high):
    def one(axis_at, shards_of):
        heights = jax.random.uniform(jax.random.fold_in(jax.random.fold_in(stream_key, 6), axis_at), (shards_of,), jnp.float32, low / len(shards), high / len(shards))
        return jnp.repeat(jnp.exp(heights), extent[axis_at] // shards_of).reshape((-1,) + (1,) * (len(extent) - axis_at - 1))

    factor_of = one(*shards[0])
    for cut in shards[1:]:
        factor_of = factor_of * one(*cut)
    return factor_of


def centred(rng, shape, scale, limit, shards=(), held_as=jnp.bfloat16):
    values = scale * jax.random.normal(rng, shape, jnp.float32)
    if shards:
        values = values * level_of(rng, shape, shards, -0.22, 0.18)
    return jnp.clip(values, -limit, limit).astype(held_as)


def setup_inputs(seed: int = 0, part: int = 0) -> dict:
    arg_keys = jax.random.split(jax.random.key(seed), 11)
    own_keys = jax.random.split(jax.random.fold_in(arg_keys[10], part), 11)
    hidden = centred(own_keys[0], (NEW, MODEL_WIDTH), 1.0, 6.0)
    w_query = centred(arg_keys[1], (MODEL_WIDTH, QUERY_HEADS * HEAD_SIZE), MODEL_WIDTH ** -0.5, 0.078125, ((1, 16),))
    key_projection_weight = centred(arg_keys[2], (MODEL_WIDTH, KEY_VALUE_HEADS * HEAD_SIZE), MODEL_WIDTH ** -0.5, 0.078125, ((1, 16),))
    value_projection_weight = centred(arg_keys[3], (MODEL_WIDTH, KEY_VALUE_HEADS * HEAD_SIZE), MODEL_WIDTH ** -0.5, 0.078125, ((1, 16),))
    query_gain = jnp.clip(jnp.exp(jax.random.uniform(arg_keys[4], (HEAD_SIZE,), jnp.float32, math.log(0.5), math.log(1.5))), 0.5, 1.5)
    key_gain = jnp.clip(jnp.exp(jax.random.uniform(arg_keys[5], (HEAD_SIZE,), jnp.float32, math.log(4.0), math.log(8.0))), 4.0, 8.0)
    stored_cache_keys = draw_stored_cache_keys(jax.random.fold_in(jax.random.fold_in(arg_keys[10], part), 71), part)
    stored_cache_values = centred(own_keys[7], (CACHE_SLOTS, KEY_VALUE_HEADS * HEAD_SIZE), 2.0, 8.0, ((0, 16),))
    cache_length = jax.random.randint(own_keys[8], (1,), CACHE_SLOTS // 2, CACHE_SLOTS + 1).astype(jnp.int32)
    first_position = jax.random.randint(own_keys[9], (1,), 0, 4096).astype(jnp.int32)
    return dict(hidden=hidden, w_query=w_query, key_projection_weight=key_projection_weight, value_projection_weight=value_projection_weight, query_gain=query_gain, key_gain=key_gain, stored_cache_keys=stored_cache_keys, stored_cache_values=stored_cache_values, cache_length=cache_length, first_position=first_position)


def normalize(joined_values, gain):
    mean_square = lax.optimization_barrier(jnp.mean(joined_values * joined_values, axis=-1, keepdims=True))
    return joined_values * lax.rsqrt(mean_square + 1e-06) * gain

def rotate(joined_values, positions):
    half = joined_values.shape[-1] // 2
    freq = jnp.exp(jnp.arange(half, dtype=jnp.float32) * (-2.0 * math.log(1000000.0) / joined_values.shape[-1]))
    angles = positions[:, None] * freq[None, :]
    cosine = jnp.concatenate([jnp.cos(angles), jnp.cos(angles)], axis=-1)[:, None, :]
    sine = jnp.concatenate([jnp.sin(angles), jnp.sin(angles)], axis=-1)[:, None, :]
    turned = jnp.concatenate([-joined_values[..., half:], joined_values[..., :half]], axis=-1)
    return joined_values * cosine + turned * sine

def reference(hidden, w_query, key_projection_weight, value_projection_weight, query_gain, key_gain, stored_cache_keys, stored_cache_values, cache_length, first_position):
    input_tokens = hidden.shape[0]
    positions = first_position[0].astype(jnp.float32) + jnp.arange(input_tokens, dtype=jnp.float32)
    projected = jnp.dot(hidden, w_query, preferred_element_type=jnp.float32).reshape(input_tokens, QUERY_HEADS, HEAD_SIZE)
    query_states = rotate(normalize(projected, query_gain), positions).astype(jnp.bfloat16)
    key_unnormalized = jnp.dot(hidden, key_projection_weight, preferred_element_type=jnp.float32).astype(jnp.bfloat16)
    key_unnormalized = lax.optimization_barrier(key_unnormalized).astype(jnp.float32).reshape(input_tokens, HEAD_SIZE, KEY_VALUE_HEADS).transpose(0, 2, 1)
    incoming_keys = rotate(normalize(key_unnormalized, key_gain), positions).astype(jnp.bfloat16)
    incoming_values = jnp.dot(hidden, value_projection_weight, preferred_element_type=jnp.float32).astype(jnp.bfloat16).reshape(input_tokens, HEAD_SIZE, KEY_VALUE_HEADS).transpose(0, 2, 1)
    query_group = QUERY_HEADS // KEY_VALUE_HEADS
    token_rows = query_states.reshape(input_tokens, KEY_VALUE_HEADS, query_group, HEAD_SIZE).transpose(1, 2, 0, 3).reshape(KEY_VALUE_HEADS, query_group * input_tokens, HEAD_SIZE)
    joined_keys = jnp.concatenate([stored_cache_keys.reshape(CACHE_SLOTS, KEY_VALUE_HEADS, HEAD_SIZE).transpose(1, 0, 2), incoming_keys.transpose(1, 0, 2)], axis=1)
    joined_values = jnp.concatenate([stored_cache_values.reshape(CACHE_SLOTS, KEY_VALUE_HEADS, HEAD_SIZE).transpose(1, 0, 2), incoming_values.transpose(1, 0, 2)], axis=1)
    cached = jnp.arange(CACHE_SLOTS) < cache_length[0]
    token_of_row = jnp.arange(query_group * input_tokens) % input_tokens
    causal = jnp.arange(input_tokens)[None, :] <= token_of_row[:, None]
    visible = jnp.concatenate([jnp.broadcast_to(cached[None, :], (query_group * input_tokens, CACHE_SLOTS)), causal], axis=1)
    scale = 1.0 / math.sqrt(HEAD_SIZE)

    def one_head(operands):
        query_rows, key_rows, value_rows = operands
        scores = lax.dot_general(query_rows, key_rows, (((1,), (1,)), ((), ())), preferred_element_type=jnp.float32) * scale
        masked = jnp.where(visible, scores, -1e+30)
        top = lax.optimization_barrier(jnp.max(masked, axis=1, keepdims=True))
        weights = jnp.where(visible, jnp.exp(masked - top), 0.0)
        total = lax.optimization_barrier(jnp.sum(weights, axis=1, keepdims=True))
        mixed = jnp.dot(weights.astype(jnp.bfloat16), value_rows, preferred_element_type=jnp.float32)
        return mixed / total
    attention_output = lax.map(one_head, (token_rows, joined_keys, joined_values))
    attention_output = attention_output.reshape(KEY_VALUE_HEADS, query_group, input_tokens, HEAD_SIZE).transpose(2, 0, 1, 3).reshape(input_tokens, QUERY_HEADS * HEAD_SIZE)
    return attention_output.astype(jnp.bfloat16)
```

```python
import functools
import math

import jax
import jax.numpy as jnp
from jax import lax
from jax.experimental import pallas as pl
from jax.experimental.pallas import tpu as pltpu
from jax.sharding import PartitionSpec as P

MESH = pl.DeviceIdType.MESH
LOW = -1e30
FLOOR = -1e29
NT = (((1,), (1,)), ((), ()))


def log2_of(value):
    bits = value.bit_length() - 1
    assert 1 << bits == value
    return bits


def flip(index, mask):
    out = index
    bit = 0
    while mask >> bit:
        if (mask >> bit) & 1:
            weight = 1 << bit
            out = out + weight * (1 - 2 * lax.rem(lax.div(index, weight), 2))
        bit += 1
    return out


def one_hot(target, columns):
    ids = lax.broadcasted_iota(jnp.int32, (target.shape[0], columns), 1)
    return jnp.where(ids == target, 1.0, 0.0).astype(jnp.bfloat16)


def kernel(
    groups,
    kv_heads,
    hidden_hbm,
    wq_hbm,
    wk_hbm,
    wv_hbm,
    query_gain_hbm,
    key_gain_hbm,
    keys_hbm,
    values_hbm,
    length_hbm,
    first_hbm,
    out,
    hid,
    wq,
    wkv,
    stage,
    held,
    slab_out,
    slab_in,
    queries,
    query_gain,
    key_gain,
    length,
    first,
    load_sem,
    wq_sem,
    own_sem,
    send_sem,
    recv_sem,
    pass_sem,
    passed_sem,
    slab_send,
    slab_recv,
    slab_pass,
    slab_passed,
    late_sem,
):
    me = lax.axis_index("ctx")
    core, chip = lax.rem(me, 2), lax.div(me, 2)
    chips = groups // 2
    sharers = groups // kv_heads
    tokens, width = hid.shape
    head_dim = query_gain.shape[1]
    heads_here = wq.shape[1] // head_dim
    slots = stage.shape[1]
    columns = wkv.shape[0] // 2
    depth = columns // kv_heads
    rows = slab_out.shape[1]
    half = head_dim // 2
    scale = math.log2(math.e) / math.sqrt(head_dim)

    barrier = pltpu.get_barrier_semaphore()
    sibling = chip * 2 + (1 - core)
    last_plane = lax.div(chip, chips - 2)

    def greet(semaphore, peer):
        pl.semaphore_signal(semaphore, inc=1, device_id={"ctx": peer}, device_id_type=MESH)

    @pl.when(last_plane == 0)
    def _():
        for mask in reversed(range(2, chips)):
            greet(barrier, flip(chip, mask) * 2 + core)

    greet(barrier, flip(chip, 1) * 2 + core)
    greet(barrier, sibling)

    small_loads = [
        pltpu.make_async_copy(first_hbm, first, load_sem.at[5]),
        pltpu.make_async_copy(length_hbm, length, load_sem.at[6]),
        pltpu.make_async_copy(query_gain_hbm, query_gain, load_sem.at[7]),
        pltpu.make_async_copy(key_gain_hbm, key_gain, load_sem.at[8]),
    ]
    state_loads = [
        pltpu.make_async_copy(hidden_hbm, hid, load_sem.at[2]),
        pltpu.make_async_copy(wk_hbm, wkv.at[pl.ds(0, columns)], load_sem.at[3]),
        pltpu.make_async_copy(wv_hbm, wkv.at[pl.ds(columns, columns)], load_sem.at[4]),
    ]
    cache_loads = [
        pltpu.make_async_copy(keys_hbm, stage.at[0], load_sem.at[0]),
        pltpu.make_async_copy(values_hbm, stage.at[1], load_sem.at[1]),
    ]
    for load in cache_loads + state_loads + small_loads:
        load.start()
    wide = min(2 * head_dim, wq.shape[1])
    wq_loads = []
    for part in range(wq.shape[1] // wide):
        cut = pl.ds(part * wide, wide)
        wq_loads.append(
            pltpu.make_async_copy(wq_hbm.at[:, cut], wq.at[:, cut], wq_sem.at[part])
        )

    def block_of(device):
        offset = pl.multiple_of((device // sharers) * head_dim, head_dim)
        return stage.at[:, :, pl.ds(offset, head_dim)]

    last = chips - 1
    middle = chips // 2
    low, high = lax.rem(lax.div(chip, 2), 2), lax.div(chip, middle)
    orders = [list(range(chips))] * 4
    if chips == 8:
        orders = [
            [0, 1, 6, 7, 2, 3, 4, 5],
            [0, 1, 2, 3, 4, 5, 6, 7],
            [0, 1, 4, 6, 5, 2, 3, 7],
            [0, 1, 2, 3, 6, 7, 4, 5],
        ]
    picks = [(1 - low) * (1 - high), low * (1 - high), (1 - low) * high, low * high]

    def by_place(values):
        return sum(pick * value for pick, value in zip(picks, values))

    def mask_of(step):
        masks = [order[step] for order in orders] if step < chips else [chips]
        return masks[0] if len(set(masks)) == 1 else by_place(masks)

    def chip_of(step):
        masks = [order[step] for order in orders]
        if len(set(masks)) == 1:
            return flip(chip, masks[0])
        return by_place([flip(chip, mask) for mask in masks])

    def sent(mask, to):
        peer = to * 2 + core
        return pltpu.make_async_remote_copy(
            src_ref=block_of(peer),
            dst_ref=held.at[mask, :, pl.ds(0, slots)],
            send_sem=send_sem.at[mask],
            recv_sem=recv_sem.at[mask],
            device_id={"ctx": peer},
            device_id_type=MESH,
        )

    def arriving(step):
        mask = mask_of(step)
        place = held.at[mask, :, pl.ds(0, slots)]
        return pltpu.make_async_copy(place, place, recv_sem.at[mask])

    def forwarded(step):
        if step == 0:
            source = block_of(sibling)
        else:
            source = held.at[mask_of(step), :, pl.ds(0, slots)]
        return pltpu.make_async_remote_copy(
            src_ref=source,
            dst_ref=held.at[mask_of(step + 1), :, pl.ds(slots, slots)],
            send_sem=pass_sem.at[step],
            recv_sem=passed_sem.at[step],
            device_id={"ctx": sibling},
            device_id_type=MESH,
        )

    to_even = [
        sent(mask + 2 * low, flip(chip, mask) - 2 * low)
        for mask in range(middle, chips)
        if not mask & 2
    ]
    to_odd = [
        sent(mask + 2 - 2 * low, flip(chip, mask) - 2 * low + 2)
        for mask in range(middle, chips)
        if not mask & 2
    ]
    nearest = sent(1, flip(chip, 1))
    near = [sent(mask, flip(chip, mask)) for mask in range(2, middle)]
    passes = {step: forwarded(step) for step in range(chips)}

    for load in cache_loads:
        load.wait()
    own = pltpu.make_async_copy(block_of(me), held.at[0, :, pl.ds(0, slots)], own_sem.at[0])
    own.start()
    for load in wq_loads:
        load.start()

    pl.semaphore_wait(barrier, chips - 2 + 2 * last_plane)

    @pl.when(last_plane == 1)
    def _():
        for mask in range(2, chips):
            greet(late_sem, flip(chip, mask) * 2 + core)

    for send in to_even[:1] + [nearest]:
        send.start()

    for load in state_loads:
        load.wait()
    states = hid[...]
    raw = lax.dot_general(
        wkv[...], states, NT, preferred_element_type=jnp.float32
    ).astype(jnp.bfloat16)
    row = lax.broadcasted_iota(jnp.int32, (kv_heads * rows, 1), 0)
    head, inner = row >> log2_of(rows), row & (rows - 1)
    which, deep = inner >> log2_of(depth), inner & (depth - 1)
    target = jnp.where(which < 2, which * columns + deep * kv_heads + head, -1)
    regrouped = jnp.dot(one_hot(target, 2 * columns), raw, preferred_element_type=jnp.float32)
    for head_id in range(kv_heads):
        slab_out[head_id] = regrouped[head_id * rows : (head_id + 1) * rows].astype(jnp.bfloat16)

    own_slab = pltpu.make_async_copy(
        slab_out.at[me // sharers], slab_in.at[core, chip], own_sem.at[1]
    )
    own_slab.start()

    def slab_to(mask, to):
        peer = to * 2 + core
        return pltpu.make_async_remote_copy(
            src_ref=slab_out.at[peer // sharers],
            dst_ref=slab_in.at[core, chip],
            send_sem=slab_send.at[mask],
            recv_sem=slab_recv.at[mask],
            device_id={"ctx": peer},
            device_id_type=MESH,
        )

    slabs = [slab_to(mask, flip(chip, mask)) for mask in range(1, chips)]
    slabs_even = [
        slab_to(mask + 2 * low, flip(chip, mask) - 2 * low)
        for mask in range(middle, chips)
        if not mask & 2
    ]
    slabs_odd = [
        slab_to(mask + 2 - 2 * low, flip(chip, mask) - 2 * low + 2)
        for mask in range(middle, chips)
        if not mask & 2
    ]

    for send in slabs[:1] + slabs_even:
        send.start()

    @pl.when(high == 0)
    def _():
        for send in slabs[1 : middle - 1] + near:
            send.start()

    @pl.when(last_plane == 0)
    def _():
        pl.semaphore_wait(late_sem, 2)

    for send in slabs_odd:
        send.start()

    @pl.when(high == 1)
    def _():
        for send in slabs[1 : middle - 1]:
            send.start()

    for send in to_even[1:]:
        send.start()

    @pl.when(high == 1)
    def _():
        for send in near:
            send.start()

    for send in to_odd:
        send.start()

    passes[0].start()

    slab_passed_on = pltpu.make_async_remote_copy(
        src_ref=slab_in.at[core],
        dst_ref=slab_in.at[core],
        send_sem=slab_pass.at[0],
        recv_sem=slab_passed.at[0],
        device_id={"ctx": sibling},
        device_id_type=MESH,
    )
    for load in small_loads:
        load.wait()
    angle_row = lax.broadcasted_iota(jnp.int32, (half, tokens), 0).astype(jnp.float32)
    freq = jnp.exp(angle_row * (-2.0 * math.log(1000000.0) / head_dim))
    token_id = lax.broadcasted_iota(jnp.int32, (half, tokens), 1).astype(jnp.float32)
    angles = (first[0].astype(jnp.float32) + token_id) * freq
    cos_t, sin_t = jnp.cos(angles), jnp.sin(angles)
    table = jnp.concatenate([cos_t, sin_t], axis=0).T
    turned_table = pltpu.roll(table, half, 1)
    low_lane = lax.broadcasted_iota(jnp.int32, (tokens, head_dim), 1) < half
    cos_q = jnp.where(low_lane, table, turned_table)
    sin_q = jnp.where(low_lane, -turned_table, table)

    gain = query_gain[...]
    per_part = wide // head_dim
    for part, load in enumerate(wq_loads):
        load.wait()
        projected = jnp.dot(
            states, wq[:, part * wide : (part + 1) * wide], preferred_element_type=jnp.float32
        )
        for local in range(per_part):
            value = projected[:, local * head_dim : (local + 1) * head_dim]
            mean_square = jnp.mean(value * value, axis=1, keepdims=True)
            value = value * lax.rsqrt(mean_square + 1e-06) * gain
            value = value * cos_q + pltpu.roll(value, half, 1) * sin_q
            at = (part * per_part + local) * tokens
            queries[at : at + tokens] = value.astype(jnp.bfloat16)

    state = [None] * heads_here

    def attend(key_rows, value_rows, bias, keys_across=False):
        for head_id in range(heads_here):
            query = queries[head_id * tokens : (head_id + 1) * tokens]
            if keys_across:
                scores = jnp.dot(query, key_rows, preferred_element_type=jnp.float32)
            else:
                scores = lax.dot_general(query, key_rows, NT, preferred_element_type=jnp.float32)
            scores = scores + bias
            top = jnp.max(scores, axis=1, keepdims=True)
            old = state[head_id]
            top = jnp.maximum(top, FLOOR if old is None else old[1])
            weights = jnp.exp2((scores - top) * scale)
            total = jnp.sum(weights, axis=1, keepdims=True)
            weights = weights.astype(jnp.bfloat16)
            if keys_across:
                summed = lax.dot_general(
                    weights, value_rows, NT, preferred_element_type=jnp.float32
                )
            else:
                summed = jnp.dot(weights, value_rows, preferred_element_type=jnp.float32)
            if old is not None:
                fade = jnp.exp2((old[1] - top) * scale)
                summed = summed + old[0] * fade
                total = total + old[2] * fade
            state[head_id] = (summed, top, total)

    def attend_step(step):
        start = slots if step == chips else 0
        stop = slots if step == 0 else 2 * slots
        count = stop - start
        lane = lax.broadcasted_iota(jnp.int32, (1, count), 1) + start
        here = chip_of(min(step, last)) * 2 + core
        other = chip_of(max(step - 1, 0)) * 2 + 1 - core
        source = jnp.where(lane < slots, here, other)
        position = source * slots + (lane & (slots - 1))
        bias = jnp.where(position < length[0], 0.0, LOW)
        span = pl.ds(start, count)
        at = mask_of(step)
        attend(held[at, 0, span], held[at, 1, span], bias)

    def attend_new():
        slab_passed_on.wait_recv()
        pick = lax.broadcasted_iota(jnp.int32, (2 * head_dim, 1), 0)
        kind, entry = pick >> log2_of(head_dim), pick & (head_dim - 1)
        source, deep = entry >> log2_of(depth), entry & (depth - 1)
        place = (source & 1) * chips + (source >> 1)
        joined = jnp.dot(
            one_hot(place * rows + kind * depth + deep, groups * rows),
            slab_in[...].reshape(groups * rows, tokens),
            preferred_element_type=jnp.float32,
        )
        key_raw = joined[:head_dim]
        value_new = joined[head_dim:].astype(jnp.bfloat16)
        gain_rows = jnp.broadcast_to(key_gain[...], (tokens, head_dim)).T
        mean_square = jnp.mean(key_raw * key_raw, axis=0, keepdims=True)
        normed = key_raw * lax.rsqrt(mean_square + 1e-06) * gain_rows
        upper, lower = normed[:half], normed[half:]
        key_new = jnp.concatenate(
            [upper * cos_t - lower * sin_t, lower * cos_t + upper * sin_t], axis=0
        ).astype(jnp.bfloat16)
        seen = lax.broadcasted_iota(jnp.int32, (tokens, tokens), 1)
        asks = lax.broadcasted_iota(jnp.int32, (tokens, tokens), 0)
        attend(key_new, value_new, jnp.where(seen <= asks, 0.0, LOW), keys_across=True)

    own.wait()
    attend_step(0)
    for step in range(1, chips):
        arriving(step).wait()
        passes[step].start()
        if step == 3:
            own_slab.wait()
            for slab_copy in slabs:
                slab_copy.wait_recv()
            slab_passed_on.start()
        if step == 4:
            attend_new()
        passes[step - 1].wait_recv()
        attend_step(step)
    passes[last].wait_recv()
    attend_step(chips)

    for head_id in range(heads_here):
        summed, _, total = state[head_id]
        out[:, head_id * head_dim : (head_id + 1) * head_dim] = (summed / total).astype(
            jnp.bfloat16
        )

    for send in to_even + to_odd + [nearest] + near:
        send.wait_send()
    for step in range(chips):
        passes[step].wait_send()
    for slab_copy in slabs + [slab_passed_on]:
        slab_copy.wait_send()


def per_device(
    hidden,
    w_query,
    key_projection_weight,
    value_projection_weight,
    query_gain,
    key_gain,
    stored_cache_keys,
    stored_cache_values,
    cache_length,
    first_position,
):
    groups = lax.axis_size("ctx")
    tokens, width = hidden.shape
    head_dim = query_gain.shape[0]
    kv_heads = stored_cache_keys.shape[1] // head_dim
    slots = stored_cache_keys.shape[0]
    columns = key_projection_weight.shape[1]
    own_width = w_query.shape[1]
    rows = max(16, 2 * (columns // kv_heads))
    chips = groups // 2
    anywhere = pl.BlockSpec(memory_space=pltpu.HBM)
    vmem = pl.BlockSpec(memory_space=pltpu.VMEM)
    bf16 = jnp.bfloat16
    dma = pltpu.SemaphoreType.DMA
    return pl.pallas_call(
        functools.partial(kernel, groups, kv_heads),
        out_shape=pltpu.VMEM((tokens, own_width), bf16),
        in_specs=[anywhere] * 10,
        out_specs=vmem,
        scratch_shapes=[
            pltpu.VMEM((tokens, width), bf16),
            pltpu.VMEM((width, own_width), bf16),
            pltpu.VMEM((2 * columns, width), bf16),
            pltpu.VMEM((2, slots, kv_heads * head_dim), bf16),
            pltpu.VMEM((chips + 1, 2, 2 * slots, head_dim), bf16),
            pltpu.VMEM((kv_heads, rows, tokens), bf16),
            pltpu.VMEM((2, chips, rows, tokens), bf16),
            pltpu.VMEM((own_width // head_dim * tokens, head_dim), bf16),
            pltpu.VMEM((1, head_dim), jnp.float32),
            pltpu.VMEM((1, head_dim), jnp.float32),
            pltpu.SMEM((1,), jnp.int32),
            pltpu.SMEM((1,), jnp.int32),
            dma((9,)),
            dma((max(1, own_width // head_dim),)),
            dma((2,)),
            dma((chips,)),
            dma((chips,)),
            dma((chips,)),
            dma((chips,)),
            dma((chips,)),
            dma((chips,)),
            dma((chips,)),
            dma((chips,)),
            pltpu.SemaphoreType.REGULAR,
        ],
        compiler_params=pltpu.CompilerParams(collective_id=0, has_side_effects=True),
    )(
        hidden,
        w_query,
        key_projection_weight.T,
        value_projection_weight.T,
        query_gain.reshape(1, head_dim),
        key_gain.reshape(1, head_dim),
        stored_cache_keys,
        stored_cache_values,
        cache_length,
        first_position,
    )


def solution(mesh):
    return jax.shard_map(
        per_device,
        mesh=mesh,
        in_specs=(
            P("req", None),
            P(None, "ctx"),
            P(None, "ctx"),
            P(None, "ctx"),
            P(),
            P(),
            P(("req", "ctx"), None),
            P(("req", "ctx"), None),
            P("req"),
            P("req"),
        ),
        out_specs=P("req", "ctx"),
        check_vma=False,
    )
```

```python
import functools
import math

import jax
import jax.numpy as jnp
from jax import lax
from jax.experimental import pallas as pl
from jax.experimental.pallas import tpu as pltpu
from jax.sharding import PartitionSpec as P

MESH = pl.DeviceIdType.MESH
LOW = -1e30
FLOOR = -1e29
NT = (((1,), (1,)), ((), ()))


def log2_of(value):
    bits = value.bit_length() - 1
    assert 1 << bits == value
    return bits


def flip(index, mask):
    out = index
    bit = 0
    while mask >> bit:
        if (mask >> bit) & 1:
            weight = 1 << bit
            out = out + weight * (1 - 2 * lax.rem(lax.div(index, weight), 2))
        bit += 1
    return out


def one_hot(target, columns):
    ids = lax.broadcasted_iota(jnp.int32, (target.shape[0], columns), 1)
    return jnp.where(ids == target, 1.0, 0.0).astype(jnp.bfloat16)


def kernel(
    groups,
    kv_heads,
    hidden_hbm,
    wq_hbm,
    wk_hbm,
    wv_hbm,
    query_gain_hbm,
    key_gain_hbm,
    keys_hbm,
    values_hbm,
    length_hbm,
    first_hbm,
    out,
    hid,
    wq,
    wkv,
    stage,
    held,
    slab_out,
    slab_in,
    queries,
    query_gain,
    key_gain,
    length,
    first,
    load_sem,
    wq_sem,
    own_sem,
    send_sem,
    recv_sem,
    pass_sem,
    passed_sem,
    slab_send,
    slab_recv,
    slab_pass,
    slab_passed,
    late_sem,
):
    me = lax.axis_index("ctx")
    core, chip = lax.rem(me, 2), lax.div(me, 2)
    chips = groups // 2
    sharers = groups // kv_heads
    tokens, width = hid.shape
    head_dim = query_gain.shape[1]
    heads_here = wq.shape[1] // head_dim
    slots = stage.shape[1]
    columns = wkv.shape[0] // 2
    depth = columns // kv_heads
    rows = slab_out.shape[1]
    half = head_dim // 2
    scale = math.log2(math.e) / math.sqrt(head_dim)

    barrier = pltpu.get_barrier_semaphore()
    sibling = chip * 2 + (1 - core)
    last_plane = lax.div(chip, chips - 2)

    def greet(semaphore, peer):
        pl.semaphore_signal(semaphore, inc=1, device_id={"ctx": peer}, device_id_type=MESH)

    @pl.when(last_plane == 0)
    def _():
        for mask in reversed(range(2, chips)):
            greet(barrier, flip(chip, mask) * 2 + core)

    greet(barrier, flip(chip, 1) * 2 + core)
    greet(barrier, sibling)

    small_loads = [
        pltpu.make_async_copy(first_hbm, first, load_sem.at[5]),
        pltpu.make_async_copy(length_hbm, length, load_sem.at[6]),
        pltpu.make_async_copy(query_gain_hbm, query_gain, load_sem.at[7]),
        pltpu.make_async_copy(key_gain_hbm, key_gain, load_sem.at[8]),
    ]
    state_loads = [
        pltpu.make_async_copy(hidden_hbm, hid, load_sem.at[2]),
        pltpu.make_async_copy(wk_hbm, wkv.at[pl.ds(0, columns)], load_sem.at[3]),
        pltpu.make_async_copy(wv_hbm, wkv.at[pl.ds(columns, columns)], load_sem.at[4]),
    ]
    cache_loads = [
        pltpu.make_async_copy(keys_hbm, stage.at[0], load_sem.at[0]),
        pltpu.make_async_copy(values_hbm, stage.at[1], load_sem.at[1]),
    ]
    for load in cache_loads + state_loads + small_loads:
        load.start()
    wide = min(2 * head_dim, wq.shape[1])
    wq_loads = []
    for part in range(wq.shape[1] // wide):
        cut = pl.ds(part * wide, wide)
        wq_loads.append(
            pltpu.make_async_copy(wq_hbm.at[:, cut], wq.at[:, cut], wq_sem.at[part])
        )

    def block_of(device):
        offset = pl.multiple_of((device // sharers) * head_dim, head_dim)
        return stage.at[:, :, pl.ds(offset, head_dim)]

    last = chips - 1
    middle = chips // 2
    low, high = lax.rem(lax.div(chip, 2), 2), lax.div(chip, middle)
    orders = [list(range(chips))] * 4
    if chips == 8:
        orders = [
            [0, 1, 6, 7, 2, 4, 3, 5],
            [0, 1, 2, 3, 4, 5, 6, 7],
            [0, 1, 4, 6, 7, 5, 2, 3],
            [0, 1, 2, 3, 6, 7, 4, 5],
        ]
    picks = [(1 - low) * (1 - high), low * (1 - high), (1 - low) * high, low * high]

    def by_place(values):
        return sum(pick * value for pick, value in zip(picks, values))

    def mask_of(step):
        masks = [order[step] for order in orders] if step < chips else [chips]
        return masks[0] if len(set(masks)) == 1 else by_place(masks)

    def chip_of(step):
        masks = [order[step] for order in orders]
        if len(set(masks)) == 1:
            return flip(chip, masks[0])
        return by_place([flip(chip, mask) for mask in masks])

    def sent(mask, to):
        peer = to * 2 + core
        return pltpu.make_async_remote_copy(
            src_ref=block_of(peer),
            dst_ref=held.at[mask, :, pl.ds(0, slots)],
            send_sem=send_sem.at[mask],
            recv_sem=recv_sem.at[mask],
            device_id={"ctx": peer},
            device_id_type=MESH,
        )

    def arriving(step):
        mask = mask_of(step)
        place = held.at[mask, :, pl.ds(0, slots)]
        return pltpu.make_async_copy(place, place, recv_sem.at[mask])

    def forwarded(step):
        if step == 0:
            source = block_of(sibling)
        else:
            source = held.at[mask_of(step), :, pl.ds(0, slots)]
        return pltpu.make_async_remote_copy(
            src_ref=source,
            dst_ref=held.at[mask_of(step + 1), :, pl.ds(slots, slots)],
            send_sem=pass_sem.at[step],
            recv_sem=passed_sem.at[step],
            device_id={"ctx": sibling},
            device_id_type=MESH,
        )

    to_even = [
        sent(mask + 2 * low, flip(chip, mask) - 2 * low)
        for mask in range(middle, chips)
        if not mask & 2
    ]
    to_odd = [
        sent(mask + 2 - 2 * low, flip(chip, mask) - 2 * low + 2)
        for mask in range(middle, chips)
        if not mask & 2
    ]
    nearest = sent(1, flip(chip, 1))
    near = [sent(mask, flip(chip, mask)) for mask in range(2, middle)]
    passes = {step: forwarded(step) for step in range(chips)}

    for load in cache_loads:
        load.wait()
    own = pltpu.make_async_copy(block_of(me), held.at[0, :, pl.ds(0, slots)], own_sem.at[0])
    own.start()
    for load in wq_loads:
        load.start()

    pl.semaphore_wait(barrier, chips - 2 + 2 * last_plane)

    @pl.when(last_plane == 1)
    def _():
        for mask in range(2, chips):
            greet(late_sem, flip(chip, mask) * 2 + core)

    for send in to_even[:1] + [nearest]:
        send.start()

    for load in state_loads:
        load.wait()
    states = hid[...]
    raw = lax.dot_general(
        wkv[...], states, NT, preferred_element_type=jnp.float32
    ).astype(jnp.bfloat16)
    row = lax.broadcasted_iota(jnp.int32, (kv_heads * rows, 1), 0)
    head, inner = row >> log2_of(rows), row & (rows - 1)
    which, deep = inner >> log2_of(depth), inner & (depth - 1)
    target = jnp.where(which < 2, which * columns + deep * kv_heads + head, -1)
    regrouped = jnp.dot(one_hot(target, 2 * columns), raw, preferred_element_type=jnp.float32)
    for head_id in range(kv_heads):
        slab_out[head_id] = regrouped[head_id * rows : (head_id + 1) * rows].astype(jnp.bfloat16)

    own_slab = pltpu.make_async_copy(
        slab_out.at[me // sharers], slab_in.at[core, chip], own_sem.at[1]
    )
    own_slab.start()

    def slab_to(mask, to):
        peer = to * 2 + core
        return pltpu.make_async_remote_copy(
            src_ref=slab_out.at[peer // sharers],
            dst_ref=slab_in.at[core, chip],
            send_sem=slab_send.at[mask],
            recv_sem=slab_recv.at[mask],
            device_id={"ctx": peer},
            device_id_type=MESH,
        )

    slabs = [slab_to(mask, flip(chip, mask)) for mask in range(1, chips)]
    slabs_even = [
        slab_to(mask + 2 * low, flip(chip, mask) - 2 * low)
        for mask in range(middle, chips)
        if not mask & 2
    ]
    slabs_odd = [
        slab_to(mask + 2 - 2 * low, flip(chip, mask) - 2 * low + 2)
        for mask in range(middle, chips)
        if not mask & 2
    ]

    for send in slabs[:1] + slabs_even:
        send.start()

    @pl.when(high == 0)
    def _():
        for send in slabs[1 : middle - 1] + near:
            send.start()

    @pl.when(last_plane == 0)
    def _():
        pl.semaphore_wait(late_sem, 2)

    for send in slabs_odd:
        send.start()

    @pl.when(high == 1)
    def _():
        for send in slabs[1 : middle - 1]:
            send.start()

    for send in to_even[1:]:
        send.start()

    @pl.when(high == 1)
    def _():
        for send in near:
            send.start()

    for send in to_odd:
        send.start()

    passes[0].start()

    slab_passed_on = pltpu.make_async_remote_copy(
        src_ref=slab_in.at[core],
        dst_ref=slab_in.at[core],
        send_sem=slab_pass.at[0],
        recv_sem=slab_passed.at[0],
        device_id={"ctx": sibling},
        device_id_type=MESH,
    )
    for load in small_loads:
        load.wait()
    angle_row = lax.broadcasted_iota(jnp.int32, (half, tokens), 0).astype(jnp.float32)
    freq = jnp.exp(angle_row * (-2.0 * math.log(1000000.0) / head_dim))
    token_id = lax.broadcasted_iota(jnp.int32, (half, tokens), 1).astype(jnp.float32)
    angles = (first[0].astype(jnp.float32) + token_id) * freq
    cos_t, sin_t = jnp.cos(angles), jnp.sin(angles)
    table = jnp.concatenate([cos_t, sin_t], axis=0).T
    turned_table = pltpu.roll(table, half, 1)
    low_lane = lax.broadcasted_iota(jnp.int32, (tokens, head_dim), 1) < half
    cos_q = jnp.where(low_lane, table, turned_table)
    sin_q = jnp.where(low_lane, -turned_table, table)

    gain = query_gain[...]
    per_part = wide // head_dim
    for part, load in enumerate(wq_loads):
        load.wait()
        projected = jnp.dot(
            states, wq[:, part * wide : (part + 1) * wide], preferred_element_type=jnp.float32
        )
        for local in range(per_part):
            value = projected[:, local * head_dim : (local + 1) * head_dim]
            mean_square = jnp.mean(value * value, axis=1, keepdims=True)
            value = value * lax.rsqrt(mean_square + 1e-06) * gain
            value = value * cos_q + pltpu.roll(value, half, 1) * sin_q
            at = (part * per_part + local) * tokens
            queries[at : at + tokens] = value.astype(jnp.bfloat16)

    state = [None] * heads_here

    def attend(key_rows, value_rows, bias, keys_across=False):
        for head_id in range(heads_here):
            query = queries[head_id * tokens : (head_id + 1) * tokens]
            if keys_across:
                scores = jnp.dot(query, key_rows, preferred_element_type=jnp.float32)
            else:
                scores = lax.dot_general(query, key_rows, NT, preferred_element_type=jnp.float32)
            scores = scores + bias
            top = jnp.max(scores, axis=1, keepdims=True)
            old = state[head_id]
            top = jnp.maximum(top, FLOOR if old is None else old[1])
            weights = jnp.exp2((scores - top) * scale)
            total = jnp.sum(weights, axis=1, keepdims=True)
            weights = weights.astype(jnp.bfloat16)
            if keys_across:
                summed = lax.dot_general(
                    weights, value_rows, NT, preferred_element_type=jnp.float32
                )
            else:
                summed = jnp.dot(weights, value_rows, preferred_element_type=jnp.float32)
            if old is not None:
                fade = jnp.exp2((old[1] - top) * scale)
                summed = summed + old[0] * fade
                total = total + old[2] * fade
            state[head_id] = (summed, top, total)

    def attend_step(step):
        start = slots if step == chips else 0
        stop = slots if step == 0 else 2 * slots
        count = stop - start
        lane = lax.broadcasted_iota(jnp.int32, (1, count), 1) + start
        here = chip_of(min(step, last)) * 2 + core
        other = chip_of(max(step - 1, 0)) * 2 + 1 - core
        source = jnp.where(lane < slots, here, other)
        position = source * slots + (lane & (slots - 1))
        bias = jnp.where(position < length[0], 0.0, LOW)
        span = pl.ds(start, count)
        at = mask_of(step)
        attend(held[at, 0, span], held[at, 1, span], bias)

    def attend_new():
        slab_passed_on.wait_recv()
        pick = lax.broadcasted_iota(jnp.int32, (2 * head_dim, 1), 0)
        kind, entry = pick >> log2_of(head_dim), pick & (head_dim - 1)
        source, deep = entry >> log2_of(depth), entry & (depth - 1)
        place = (source & 1) * chips + (source >> 1)
        joined = jnp.dot(
            one_hot(place * rows + kind * depth + deep, groups * rows),
            slab_in[...].reshape(groups * rows, tokens),
            preferred_element_type=jnp.float32,
        )
        key_raw = joined[:head_dim]
        value_new = joined[head_dim:].astype(jnp.bfloat16)
        gain_rows = jnp.broadcast_to(key_gain[...], (tokens, head_dim)).T
        mean_square = jnp.mean(key_raw * key_raw, axis=0, keepdims=True)
        normed = key_raw * lax.rsqrt(mean_square + 1e-06) * gain_rows
        upper, lower = normed[:half], normed[half:]
        key_new = jnp.concatenate(
            [upper * cos_t - lower * sin_t, lower * cos_t + upper * sin_t], axis=0
        ).astype(jnp.bfloat16)
        seen = lax.broadcasted_iota(jnp.int32, (tokens, tokens), 1)
        asks = lax.broadcasted_iota(jnp.int32, (tokens, tokens), 0)
        attend(key_new, value_new, jnp.where(seen <= asks, 0.0, LOW), keys_across=True)

    own.wait()
    attend_step(0)
    for step in range(1, chips):
        arriving(step).wait()
        passes[step].start()
        if step == 3:
            own_slab.wait()
            for slab_copy in slabs:
                slab_copy.wait_recv()
            slab_passed_on.start()
        if step == 4:
            attend_new()
        passes[step - 1].wait_recv()
        attend_step(step)
    passes[last].wait_recv()
    attend_step(chips)

    for head_id in range(heads_here):
        summed, _, total = state[head_id]
        out[:, head_id * head_dim : (head_id + 1) * head_dim] = (summed / total).astype(
            jnp.bfloat16
        )

    for send in to_even + to_odd + [nearest] + near:
        send.wait_send()
    for step in range(chips):
        passes[step].wait_send()
    for slab_copy in slabs + [slab_passed_on]:
        slab_copy.wait_send()


def per_device(
    hidden,
    w_query,
    key_projection_weight,
    value_projection_weight,
    query_gain,
    key_gain,
    stored_cache_keys,
    stored_cache_values,
    cache_length,
    first_position,
):
    groups = lax.axis_size("ctx")
    tokens, width = hidden.shape
    head_dim = query_gain.shape[0]
    kv_heads = stored_cache_keys.shape[1] // head_dim
    slots = stored_cache_keys.shape[0]
    columns = key_projection_weight.shape[1]
    own_width = w_query.shape[1]
    rows = max(16, 2 * (columns // kv_heads))
    chips = groups // 2
    anywhere = pl.BlockSpec(memory_space=pltpu.HBM)
    vmem = pl.BlockSpec(memory_space=pltpu.VMEM)
    bf16 = jnp.bfloat16
    dma = pltpu.SemaphoreType.DMA
    return pl.pallas_call(
        functools.partial(kernel, groups, kv_heads),
        out_shape=pltpu.VMEM((tokens, own_width), bf16),
        in_specs=[anywhere] * 10,
        out_specs=vmem,
        scratch_shapes=[
            pltpu.VMEM((tokens, width), bf16),
            pltpu.VMEM((width, own_width), bf16),
            pltpu.VMEM((2 * columns, width), bf16),
            pltpu.VMEM((2, slots, kv_heads * head_dim), bf16),
            pltpu.VMEM((chips + 1, 2, 2 * slots, head_dim), bf16),
            pltpu.VMEM((kv_heads, rows, tokens), bf16),
            pltpu.VMEM((2, chips, rows, tokens), bf16),
            pltpu.VMEM((own_width // head_dim * tokens, head_dim), bf16),
            pltpu.VMEM((1, head_dim), jnp.float32),
            pltpu.VMEM((1, head_dim), jnp.float32),
            pltpu.SMEM((1,), jnp.int32),
            pltpu.SMEM((1,), jnp.int32),
            dma((9,)),
            dma((max(1, own_width // head_dim),)),
            dma((2,)),
            dma((chips,)),
            dma((chips,)),
            dma((chips,)),
            dma((chips,)),
            dma((chips,)),
            dma((chips,)),
            dma((chips,)),
            dma((chips,)),
            pltpu.SemaphoreType.REGULAR,
        ],
        compiler_params=pltpu.CompilerParams(collective_id=0, has_side_effects=True),
    )(
        hidden,
        w_query,
        key_projection_weight.T,
        value_projection_weight.T,
        query_gain.reshape(1, head_dim),
        key_gain.reshape(1, head_dim),
        stored_cache_keys,
        stored_cache_values,
        cache_length,
        first_position,
    )


def solution(mesh):
    return jax.shard_map(
        per_device,
        mesh=mesh,
        in_specs=(
            P("req", None),
            P(None, "ctx"),
            P(None, "ctx"),
            P(None, "ctx"),
            P(),
            P(),
            P(("req", "ctx"), None),
            P(("req", "ctx"), None),
            P("req"),
            P("req"),
        ),
        out_specs=P("req", "ctx"),
        check_vma=False,
    )
```

```python
import functools
import math

import jax
import jax.numpy as jnp
from jax import lax
from jax.experimental import pallas as pl
from jax.experimental.pallas import tpu as pltpu
from jax.sharding import PartitionSpec as P

MESH = pl.DeviceIdType.MESH
LOW = -1e30
FLOOR = -1e29
NT = (((1,), (1,)), ((), ()))


def log2_of(value):
    bits = value.bit_length() - 1
    assert 1 << bits == value
    return bits


def flip(index, mask):
    out = index
    bit = 0
    while mask >> bit:
        if (mask >> bit) & 1:
            weight = 1 << bit
            out = out + weight * (1 - 2 * lax.rem(lax.div(index, weight), 2))
        bit += 1
    return out


def one_hot(target, columns):
    ids = lax.broadcasted_iota(jnp.int32, (target.shape[0], columns), 1)
    return jnp.where(ids == target, 1.0, 0.0).astype(jnp.bfloat16)


class Pair:
    def __init__(self, sources, target, send, recv, peer):
        self.copies = [
            pltpu.make_async_remote_copy(
                src_ref=source,
                dst_ref=target.at[kind],
                send_sem=send,
                recv_sem=recv,
                device_id={"ctx": peer},
                device_id_type=MESH,
            )
            for kind, source in enumerate(sources)
        ]
        self.target, self.send, self.recv = target, send, recv

    def start(self):
        for copy in self.copies:
            copy.start()

    def wait_send(self):
        pltpu.make_async_copy(self.target, self.target, self.send).wait()

    def wait_recv(self):
        pltpu.make_async_copy(self.target, self.target, self.recv).wait()


def kernel(
    groups,
    kv_heads,
    hidden_hbm,
    wq_hbm,
    wk_hbm,
    wv_hbm,
    query_gain_hbm,
    key_gain_hbm,
    keys_hbm,
    values_hbm,
    length_hbm,
    first_hbm,
    out,
    hid,
    wq,
    wkv,
    held,
    slab_out,
    slab_in,
    queries,
    query_gain,
    key_gain,
    length,
    first,
    load_sem,
    wq_sem,
    own_sem,
    send_sem,
    recv_sem,
    pass_sem,
    passed_sem,
    slab_send,
    slab_recv,
    slab_pass,
    slab_passed,
    late_sem,
):
    me = lax.axis_index("ctx")
    core, chip = lax.rem(me, 2), lax.div(me, 2)
    chips = groups // 2
    sharers = groups // kv_heads
    tokens, width = hid.shape
    head_dim = query_gain.shape[1]
    heads_here = wq.shape[1] // head_dim
    slots = keys_hbm.shape[0]
    columns = wkv.shape[0] // 2
    depth = columns // kv_heads
    rows = slab_out.shape[1]
    half = head_dim // 2
    scale = math.log2(math.e) / math.sqrt(head_dim)

    barrier = pltpu.get_barrier_semaphore()
    sibling = chip * 2 + (1 - core)
    last_plane = lax.div(chip, chips - 2)

    def greet(semaphore, peer):
        pl.semaphore_signal(semaphore, inc=1, device_id={"ctx": peer}, device_id_type=MESH)

    @pl.when(last_plane == 0)
    def _():
        for mask in reversed(range(2, chips)):
            greet(barrier, flip(chip, mask) * 2 + core)

    greet(barrier, flip(chip, 1) * 2 + core)
    greet(barrier, sibling)

    small_loads = [
        pltpu.make_async_copy(first_hbm, first, load_sem.at[5]),
        pltpu.make_async_copy(length_hbm, length, load_sem.at[6]),
        pltpu.make_async_copy(query_gain_hbm, query_gain, load_sem.at[7]),
        pltpu.make_async_copy(key_gain_hbm, key_gain, load_sem.at[8]),
    ]
    state_loads = [
        pltpu.make_async_copy(hidden_hbm, hid, load_sem.at[2]),
        pltpu.make_async_copy(wk_hbm, wkv.at[pl.ds(0, columns)], load_sem.at[3]),
        pltpu.make_async_copy(wv_hbm, wkv.at[pl.ds(columns, columns)], load_sem.at[4]),
    ]
    for load in state_loads:
        load.start()
    wide = min(2 * head_dim, wq.shape[1])
    wq_loads = []
    for part in range(wq.shape[1] // wide):
        cut = pl.ds(part * wide, wide)
        wq_loads.append(
            pltpu.make_async_copy(wq_hbm.at[:, cut], wq.at[:, cut], wq_sem.at[part])
        )

    def block_of(device):
        offset = pl.multiple_of((device // sharers) * head_dim, head_dim)
        columns_of = pl.ds(offset, head_dim)
        return [keys_hbm.at[:, columns_of], values_hbm.at[:, columns_of]]

    last = chips - 1
    middle = chips // 2
    low, high = lax.rem(lax.div(chip, 2), 2), lax.div(chip, middle)
    orders = [list(range(chips))] * 4
    if chips == 8:
        orders = [
            [0, 1, 6, 7, 2, 4, 3, 5],
            [0, 1, 2, 3, 4, 5, 6, 7],
            [0, 1, 4, 6, 7, 5, 2, 3],
            [0, 1, 2, 3, 6, 7, 4, 5],
        ]
    picks = [(1 - low) * (1 - high), low * (1 - high), (1 - low) * high, low * high]

    def by_place(values):
        return sum(pick * value for pick, value in zip(picks, values))

    def mask_of(step):
        masks = [order[step] for order in orders] if step < chips else [chips]
        return masks[0] if len(set(masks)) == 1 else by_place(masks)

    def chip_of(step):
        masks = [order[step] for order in orders]
        if len(set(masks)) == 1:
            return flip(chip, masks[0])
        return by_place([flip(chip, mask) for mask in masks])

    def sent(mask, to):
        peer = to * 2 + core
        return Pair(
            block_of(peer),
            held.at[mask, :, pl.ds(0, slots)],
            send_sem.at[mask],
            recv_sem.at[mask],
            peer,
        )

    def arriving(step):
        mask = mask_of(step)
        place = held.at[mask, :, pl.ds(0, slots)]
        return pltpu.make_async_copy(place, place, recv_sem.at[mask])

    def forwarded(step):
        target = held.at[mask_of(step + 1), :, pl.ds(slots, slots)]
        if step == 0:
            return Pair(block_of(sibling), target, pass_sem.at[0], passed_sem.at[0], sibling)
        return pltpu.make_async_remote_copy(
            src_ref=held.at[mask_of(step), :, pl.ds(0, slots)],
            dst_ref=target,
            send_sem=pass_sem.at[step],
            recv_sem=passed_sem.at[step],
            device_id={"ctx": sibling},
            device_id_type=MESH,
        )

    to_even = [
        sent(mask + 2 * low, flip(chip, mask) - 2 * low)
        for mask in range(middle, chips)
        if not mask & 2
    ]
    to_odd = [
        sent(mask + 2 - 2 * low, flip(chip, mask) - 2 * low + 2)
        for mask in range(middle, chips)
        if not mask & 2
    ]
    nearest = sent(1, flip(chip, 1))
    near = [sent(mask, flip(chip, mask)) for mask in range(2, middle)]
    passes = {step: forwarded(step) for step in range(chips)}

    own = [
        pltpu.make_async_copy(block, held.at[0, kind, pl.ds(0, slots)], own_sem.at[kind])
        for kind, block in enumerate(block_of(me))
    ]
    for load in own:
        load.start()
    pl.semaphore_wait(barrier, chips - 2 + 2 * last_plane)

    @pl.when(last_plane == 1)
    def _():
        for mask in range(2, chips):
            greet(late_sem, flip(chip, mask) * 2 + core)

    for send in to_even[:1] + [nearest]:
        send.start()

    @pl.when(last_plane == 1)
    def _():
        for send in to_even[1:]:
            send.start()

    for load in state_loads:
        load.wait()
    for load in wq_loads + small_loads:
        load.start()
    states = hid[...]
    raw = lax.dot_general(
        wkv[...], states, NT, preferred_element_type=jnp.float32
    ).astype(jnp.bfloat16)
    row = lax.broadcasted_iota(jnp.int32, (kv_heads * rows, 1), 0)
    head, inner = row >> log2_of(rows), row & (rows - 1)
    which, deep = inner >> log2_of(depth), inner & (depth - 1)
    target = jnp.where(which < 2, which * columns + deep * kv_heads + head, -1)
    regrouped = jnp.dot(one_hot(target, 2 * columns), raw, preferred_element_type=jnp.float32)
    for head_id in range(kv_heads):
        slab_out[head_id] = regrouped[head_id * rows : (head_id + 1) * rows].astype(jnp.bfloat16)

    own_slab = pltpu.make_async_copy(
        slab_out.at[me // sharers], slab_in.at[core, chip], own_sem.at[2]
    )
    own_slab.start()

    def slab_to(mask, to):
        peer = to * 2 + core
        return pltpu.make_async_remote_copy(
            src_ref=slab_out.at[peer // sharers],
            dst_ref=slab_in.at[core, chip],
            send_sem=slab_send.at[mask],
            recv_sem=slab_recv.at[mask],
            device_id={"ctx": peer},
            device_id_type=MESH,
        )

    slabs = [slab_to(mask, flip(chip, mask)) for mask in range(1, chips)]
    slabs_even = [
        slab_to(mask + 2 * low, flip(chip, mask) - 2 * low)
        for mask in range(middle, chips)
        if not mask & 2
    ]
    slabs_odd = [
        slab_to(mask + 2 - 2 * low, flip(chip, mask) - 2 * low + 2)
        for mask in range(middle, chips)
        if not mask & 2
    ]

    for send in slabs[:1] + slabs_even:
        send.start()

    @pl.when(high == 0)
    def _():
        for send in slabs[1 : middle - 1] + near:
            send.start()

    @pl.when(last_plane == 0)
    def _():
        pl.semaphore_wait(late_sem, 2)

    for send in slabs_odd:
        send.start()

    @pl.when(high == 1)
    def _():
        for send in slabs[1 : middle - 1]:
            send.start()

    @pl.when(last_plane == 0)
    def _():
        for send in to_even[1:]:
            send.start()

    @pl.when(high == 1)
    def _():
        for send in near:
            send.start()

    for send in to_odd:
        send.start()

    passes[0].start()

    slab_passed_on = pltpu.make_async_remote_copy(
        src_ref=slab_in.at[core],
        dst_ref=slab_in.at[core],
        send_sem=slab_pass.at[0],
        recv_sem=slab_passed.at[0],
        device_id={"ctx": sibling},
        device_id_type=MESH,
    )
    for load in small_loads:
        load.wait()
    angle_row = lax.broadcasted_iota(jnp.int32, (half, tokens), 0).astype(jnp.float32)
    freq = jnp.exp(angle_row * (-2.0 * math.log(1000000.0) / head_dim))
    token_id = lax.broadcasted_iota(jnp.int32, (half, tokens), 1).astype(jnp.float32)
    angles = (first[0].astype(jnp.float32) + token_id) * freq
    cos_t, sin_t = jnp.cos(angles), jnp.sin(angles)
    table = jnp.concatenate([cos_t, sin_t], axis=0).T
    turned_table = pltpu.roll(table, half, 1)
    low_lane = lax.broadcasted_iota(jnp.int32, (tokens, head_dim), 1) < half
    cos_q = jnp.where(low_lane, table, turned_table)
    sin_q = jnp.where(low_lane, -turned_table, table)

    gain = query_gain[...]
    per_part = wide // head_dim
    for part, load in enumerate(wq_loads):
        load.wait()
        projected = jnp.dot(
            states, wq[:, part * wide : (part + 1) * wide], preferred_element_type=jnp.float32
        )
        for local in range(per_part):
            value = projected[:, local * head_dim : (local + 1) * head_dim]
            mean_square = jnp.mean(value * value, axis=1, keepdims=True)
            value = value * lax.rsqrt(mean_square + 1e-06) * gain
            value = value * cos_q + pltpu.roll(value, half, 1) * sin_q
            at = (part * per_part + local) * tokens
            queries[at : at + tokens] = value.astype(jnp.bfloat16)

    group = min(4, heads_here)
    state = [None] * (heads_here // group)

    def attend(key_rows, value_rows, bias, keys_across=False):
        for head_id in range(heads_here // group):
            span = group * tokens
            query = queries[head_id * span : (head_id + 1) * span]
            if keys_across:
                scores = jnp.dot(query, key_rows, preferred_element_type=jnp.float32)
            else:
                scores = lax.dot_general(query, key_rows, NT, preferred_element_type=jnp.float32)
            scores = scores + bias
            top = jnp.max(scores, axis=1, keepdims=True)
            old = state[head_id]
            top = jnp.maximum(top, FLOOR if old is None else old[1])
            weights = jnp.exp2((scores - top) * scale)
            total = jnp.sum(weights, axis=1, keepdims=True)
            weights = weights.astype(jnp.bfloat16)
            if keys_across:
                summed = lax.dot_general(
                    weights, value_rows, NT, preferred_element_type=jnp.float32
                )
            else:
                summed = jnp.dot(weights, value_rows, preferred_element_type=jnp.float32)
            if old is not None:
                fade = jnp.exp2((old[1] - top) * scale)
                summed = summed + old[0] * fade
                total = total + old[2] * fade
            state[head_id] = (summed, top, total)

    def attend_step(step):
        start = slots if step == chips else 0
        stop = slots if step == 0 else 2 * slots
        count = stop - start
        lane = lax.broadcasted_iota(jnp.int32, (1, count), 1) + start
        here = chip_of(min(step, last)) * 2 + core
        other = chip_of(max(step - 1, 0)) * 2 + 1 - core
        source = jnp.where(lane < slots, here, other)
        position = source * slots + (lane & (slots - 1))
        bias = jnp.where(position < length[0], 0.0, LOW)
        span = pl.ds(start, count)
        at = mask_of(step)
        attend(held[at, 0, span], held[at, 1, span], bias)

    def attend_new():
        slab_passed_on.wait_recv()
        pick = lax.broadcasted_iota(jnp.int32, (2 * head_dim, 1), 0)
        kind, entry = pick >> log2_of(head_dim), pick & (head_dim - 1)
        source, deep = entry >> log2_of(depth), entry & (depth - 1)
        place = (source & 1) * chips + (source >> 1)
        joined = jnp.dot(
            one_hot(place * rows + kind * depth + deep, groups * rows),
            slab_in[...].reshape(groups * rows, tokens),
            preferred_element_type=jnp.float32,
        )
        key_raw = joined[:head_dim]
        value_new = joined[head_dim:].astype(jnp.bfloat16)
        gain_rows = jnp.broadcast_to(key_gain[...], (tokens, head_dim)).T
        mean_square = jnp.mean(key_raw * key_raw, axis=0, keepdims=True)
        normed = key_raw * lax.rsqrt(mean_square + 1e-06) * gain_rows
        upper, lower = normed[:half], normed[half:]
        key_new = jnp.concatenate(
            [upper * cos_t - lower * sin_t, lower * cos_t + upper * sin_t], axis=0
        ).astype(jnp.bfloat16)
        seen = lax.broadcasted_iota(jnp.int32, (group * tokens, tokens), 1)
        asks = lax.broadcasted_iota(jnp.int32, (group * tokens, tokens), 0) & (tokens - 1)
        attend(key_new, value_new, jnp.where(seen <= asks, 0.0, LOW), keys_across=True)

    for load in own:
        load.wait()
    attend_step(0)
    for step in range(1, chips):
        arriving(step).wait()
        passes[step].start()
        if step == 3:
            own_slab.wait()
            for slab_copy in slabs:
                slab_copy.wait_recv()
            slab_passed_on.start()
        if step == 4:
            attend_new()
        passes[step - 1].wait_recv()
        attend_step(step)
    passes[last].wait_recv()
    attend_step(chips)

    for head_id in range(heads_here):
        summed, _, total = state[head_id // group]
        rows_of = slice(head_id % group * tokens, (head_id % group + 1) * tokens)
        out[:, head_id * head_dim : (head_id + 1) * head_dim] = (
            summed[rows_of] / total[rows_of]
        ).astype(jnp.bfloat16)

    for send in to_even + to_odd + [nearest] + near:
        send.wait_send()
    for step in range(chips):
        passes[step].wait_send()
    for slab_copy in slabs + [slab_passed_on]:
        slab_copy.wait_send()


def per_device(
    hidden,
    w_query,
    key_projection_weight,
    value_projection_weight,
    query_gain,
    key_gain,
    stored_cache_keys,
    stored_cache_values,
    cache_length,
    first_position,
):
    groups = lax.axis_size("ctx")
    tokens, width = hidden.shape
    head_dim = query_gain.shape[0]
    kv_heads = stored_cache_keys.shape[1] // head_dim
    slots = stored_cache_keys.shape[0]
    columns = key_projection_weight.shape[1]
    own_width = w_query.shape[1]
    rows = max(16, 2 * (columns // kv_heads))
    chips = groups // 2
    anywhere = pl.BlockSpec(memory_space=pltpu.HBM)
    vmem = pl.BlockSpec(memory_space=pltpu.VMEM)
    bf16 = jnp.bfloat16
    dma = pltpu.SemaphoreType.DMA
    return pl.pallas_call(
        functools.partial(kernel, groups, kv_heads),
        out_shape=pltpu.VMEM((tokens, own_width), bf16),
        in_specs=[anywhere] * 10,
        out_specs=vmem,
        scratch_shapes=[
            pltpu.VMEM((tokens, width), bf16),
            pltpu.VMEM((width, own_width), bf16),
            pltpu.VMEM((2 * columns, width), bf16),
            pltpu.VMEM((chips + 1, 2, 2 * slots, head_dim), bf16),
            pltpu.VMEM((kv_heads, rows, tokens), bf16),
            pltpu.VMEM((2, chips, rows, tokens), bf16),
            pltpu.VMEM((own_width // head_dim * tokens, head_dim), bf16),
            pltpu.VMEM((1, head_dim), jnp.float32),
            pltpu.VMEM((1, head_dim), jnp.float32),
            pltpu.SMEM((1,), jnp.int32),
            pltpu.SMEM((1,), jnp.int32),
            dma((9,)),
            dma((max(1, own_width // head_dim),)),
            dma((3,)),
            dma((chips,)),
            dma((chips,)),
            dma((chips,)),
            dma((chips,)),
            dma((chips,)),
            dma((chips,)),
            dma((chips,)),
            dma((chips,)),
            pltpu.SemaphoreType.REGULAR,
        ],
        compiler_params=pltpu.CompilerParams(collective_id=0, has_side_effects=True),
    )(
        hidden,
        w_query,
        key_projection_weight.T,
        value_projection_weight.T,
        query_gain.reshape(1, head_dim),
        key_gain.reshape(1, head_dim),
        stored_cache_keys,
        stored_cache_values,
        cache_length,
        first_position,
    )


def solution(mesh):
    return jax.shard_map(
        per_device,
        mesh=mesh,
        in_specs=(
            P("req", None),
            P(None, "ctx"),
            P(None, "ctx"),
            P(None, "ctx"),
            P(),
            P(),
            P(("req", "ctx"), None),
            P(("req", "ctx"), None),
            P("req"),
            P("req"),
        ),
        out_specs=P("req", "ctx"),
        check_vma=False,
    )
```

```python
import functools
import math

import jax
import jax.numpy as jnp
from jax import lax
from jax.experimental import pallas as pl
from jax.experimental.pallas import tpu as pltpu
from jax.sharding import PartitionSpec as P

MESH = pl.DeviceIdType.MESH
LOW = -1e30
FLOOR = -1e29
NT = (((1,), (1,)), ((), ()))


def log2_of(value):
    bits = value.bit_length() - 1
    assert 1 << bits == value
    return bits


def flip(index, mask):
    out = index
    bit = 0
    while mask >> bit:
        if (mask >> bit) & 1:
            weight = 1 << bit
            out = out + weight * (1 - 2 * lax.rem(lax.div(index, weight), 2))
        bit += 1
    return out


def one_hot(target, columns):
    ids = lax.broadcasted_iota(jnp.int32, (target.shape[0], columns), 1)
    return jnp.where(ids == target, 1.0, 0.0).astype(jnp.bfloat16)


class Pair:
    def __init__(self, sources, target, send, recv, peer):
        self.copies = [
            pltpu.make_async_remote_copy(
                src_ref=source,
                dst_ref=target.at[kind],
                send_sem=send,
                recv_sem=recv,
                device_id={"ctx": peer},
                device_id_type=MESH,
            )
            for kind, source in enumerate(sources)
        ]
        self.target, self.send, self.recv = target, send, recv

    def start(self):
        for copy in self.copies:
            copy.start()

    def wait_send(self):
        pltpu.make_async_copy(self.target, self.target, self.send).wait()

    def wait_recv(self):
        pltpu.make_async_copy(self.target, self.target, self.recv).wait()


def kernel(
    groups,
    kv_heads,
    hidden_hbm,
    wq_hbm,
    wk_hbm,
    wv_hbm,
    query_gain_hbm,
    key_gain_hbm,
    keys_hbm,
    values_hbm,
    length_hbm,
    first_hbm,
    out,
    hid,
    wq,
    wkv,
    held,
    slab_out,
    slab_in,
    queries,
    query_gain,
    key_gain,
    length,
    first,
    load_sem,
    wq_sem,
    own_sem,
    send_sem,
    recv_sem,
    pass_sem,
    passed_sem,
    slab_send,
    slab_recv,
    slab_pass,
    slab_passed,
    late_sem,
    raw_rows,
):
    me = lax.axis_index("ctx")
    core, chip = lax.rem(me, 2), lax.div(me, 2)
    chips = groups // 2
    sharers = groups // kv_heads
    tokens, width = hid.shape
    head_dim = query_gain.shape[1]
    heads_here = wq.shape[1] // head_dim
    slots = keys_hbm.shape[0]
    columns = wkv.shape[0] // 2
    depth = columns // kv_heads
    rows = slab_out.shape[1]
    half = head_dim // 2
    scale = math.log2(math.e) / math.sqrt(head_dim)

    barrier = pltpu.get_barrier_semaphore()
    sibling = chip * 2 + (1 - core)
    last_plane = lax.div(chip, chips - 2)

    def greet(semaphore, peer):
        pl.semaphore_signal(semaphore, inc=1, device_id={"ctx": peer}, device_id_type=MESH)

    @pl.when(last_plane == 0)
    def _():
        for mask in reversed(range(2, chips)):
            greet(barrier, flip(chip, mask) * 2 + core)

    greet(barrier, flip(chip, 1) * 2 + core)
    greet(barrier, sibling)

    small_loads = [
        pltpu.make_async_copy(first_hbm, first, load_sem.at[5]),
        pltpu.make_async_copy(length_hbm, length, load_sem.at[6]),
        pltpu.make_async_copy(query_gain_hbm, query_gain, load_sem.at[7]),
        pltpu.make_async_copy(key_gain_hbm, key_gain, load_sem.at[8]),
    ]
    state_loads = [
        pltpu.make_async_copy(hidden_hbm, hid, load_sem.at[2]),
        pltpu.make_async_copy(wk_hbm, wkv.at[pl.ds(0, columns)], load_sem.at[3]),
        pltpu.make_async_copy(wv_hbm, wkv.at[pl.ds(columns, columns)], load_sem.at[4]),
    ]
    for load in state_loads:
        load.start()
    wide = min(2 * head_dim, wq.shape[1])
    wq_loads = []
    for part in range(wq.shape[1] // wide):
        cut = pl.ds(part * wide, wide)
        wq_loads.append(
            pltpu.make_async_copy(wq_hbm.at[:, cut], wq.at[:, cut], wq_sem.at[part])
        )

    def block_of(device):
        offset = pl.multiple_of((device // sharers) * head_dim, head_dim)
        columns_of = pl.ds(offset, head_dim)
        return [keys_hbm.at[:, columns_of], values_hbm.at[:, columns_of]]

    last = chips - 1
    middle = chips // 2
    low, high = lax.rem(lax.div(chip, 2), 2), lax.div(chip, middle)
    orders = [list(range(chips))] * 4
    if chips == 8:
        orders = [
            [0, 1, 6, 7, 4, 5, 2, 3],
            [0, 1, 2, 3, 4, 5, 6, 7],
            [0, 1, 4, 6, 7, 2, 5, 3],
            [0, 1, 2, 3, 6, 7, 4, 5],
        ]
    picks = [(1 - low) * (1 - high), low * (1 - high), (1 - low) * high, low * high]

    def by_place(values):
        return sum(pick * value for pick, value in zip(picks, values))

    def mask_of(step):
        masks = [order[step] for order in orders] if step < chips else [chips]
        return masks[0] if len(set(masks)) == 1 else by_place(masks)

    def chip_of(step):
        masks = [order[step] for order in orders]
        if len(set(masks)) == 1:
            return flip(chip, masks[0])
        return by_place([flip(chip, mask) for mask in masks])

    def sent(mask, to):
        peer = to * 2 + core
        return Pair(
            block_of(peer),
            held.at[mask, :, pl.ds(0, slots)],
            send_sem.at[mask],
            recv_sem.at[mask],
            peer,
        )

    def arriving(step):
        mask = mask_of(step)
        place = held.at[mask, :, pl.ds(0, slots)]
        return pltpu.make_async_copy(place, place, recv_sem.at[mask])

    def forwarded(step):
        target = held.at[mask_of(step + 1), :, pl.ds(slots, slots)]
        if step == 0:
            return Pair(block_of(sibling), target, pass_sem.at[0], passed_sem.at[0], sibling)
        return pltpu.make_async_remote_copy(
            src_ref=held.at[mask_of(step), :, pl.ds(0, slots)],
            dst_ref=target,
            send_sem=pass_sem.at[step],
            recv_sem=passed_sem.at[step],
            device_id={"ctx": sibling},
            device_id_type=MESH,
        )

    to_even = [
        sent(mask + 2 * low, flip(chip, mask) - 2 * low)
        for mask in range(middle, chips)
        if not mask & 2
    ]
    to_odd = [
        sent(mask + 2 - 2 * low, flip(chip, mask) - 2 * low + 2)
        for mask in range(middle, chips)
        if not mask & 2
    ]
    nearest = sent(1, flip(chip, 1))
    near = [sent(mask, flip(chip, mask)) for mask in range(2, middle)]
    passes = {step: forwarded(step) for step in range(chips)}

    own = [
        pltpu.make_async_copy(block, held.at[0, kind, pl.ds(0, slots)], own_sem.at[kind])
        for kind, block in enumerate(block_of(me))
    ]
    for load in own:
        load.start()
    pl.semaphore_wait(barrier, chips - 2 + 2 * last_plane)

    @pl.when(last_plane == 1)
    def _():
        for mask in range(2, chips):
            greet(late_sem, flip(chip, mask) * 2 + core)

    for send in to_even[:1] + [nearest]:
        send.start()

    @pl.when(last_plane == 1)
    def _():
        for send in to_even[1:]:
            send.start()

    for load in state_loads:
        load.wait()
    for load in wq_loads + small_loads:
        load.start()
    states = hid[...]
    raw = lax.dot_general(
        wkv[...], states, NT, preferred_element_type=jnp.float32
    ).astype(jnp.bfloat16)
    raw_rows[...] = raw.astype(jnp.float32)
    for head_id in range(kv_heads):
        slab = raw_rows[pl.ds(head_id, 2 * depth, stride=kv_heads)]
        if 2 * depth < rows:
            slab = jnp.concatenate(
                [slab, jnp.zeros((rows - 2 * depth, tokens), jnp.float32)], axis=0
            )
        slab_out[head_id] = slab.astype(jnp.bfloat16)

    own_slab = pltpu.make_async_copy(
        slab_out.at[me // sharers], slab_in.at[core, chip], own_sem.at[2]
    )
    own_slab.start()

    def slab_to(mask, to):
        peer = to * 2 + core
        return pltpu.make_async_remote_copy(
            src_ref=slab_out.at[peer // sharers],
            dst_ref=slab_in.at[core, chip],
            send_sem=slab_send.at[mask],
            recv_sem=slab_recv.at[mask],
            device_id={"ctx": peer},
            device_id_type=MESH,
        )

    slabs = [slab_to(mask, flip(chip, mask)) for mask in range(1, chips)]
    slabs_even = [
        slab_to(mask + 2 * low, flip(chip, mask) - 2 * low)
        for mask in range(middle, chips)
        if not mask & 2
    ]
    slabs_odd = [
        slab_to(mask + 2 - 2 * low, flip(chip, mask) - 2 * low + 2)
        for mask in range(middle, chips)
        if not mask & 2
    ]

    for send in slabs[:1] + slabs_even:
        send.start()

    @pl.when(high == 0)
    def _():
        for send in slabs[1 : middle - 1] + near:
            send.start()

    @pl.when(last_plane == 0)
    def _():
        pl.semaphore_wait(late_sem, 2)

    for send in slabs_odd:
        send.start()

    @pl.when(high == 1)
    def _():
        for send in slabs[1 : middle - 1]:
            send.start()

    @pl.when(last_plane == 0)
    def _():
        for send in to_even[1:]:
            send.start()

    @pl.when(high == 1)
    def _():
        for send in near:
            send.start()

    for send in to_odd:
        send.start()

    passes[0].start()

    slab_passed_on = pltpu.make_async_remote_copy(
        src_ref=slab_in.at[core],
        dst_ref=slab_in.at[core],
        send_sem=slab_pass.at[0],
        recv_sem=slab_passed.at[0],
        device_id={"ctx": sibling},
        device_id_type=MESH,
    )
    for load in small_loads:
        load.wait()
    angle_row = lax.broadcasted_iota(jnp.int32, (half, tokens), 0).astype(jnp.float32)
    freq = jnp.exp(angle_row * (-2.0 * math.log(1000000.0) / head_dim))
    token_id = lax.broadcasted_iota(jnp.int32, (half, tokens), 1).astype(jnp.float32)
    angles = (first[0].astype(jnp.float32) + token_id) * freq
    cos_t, sin_t = jnp.cos(angles), jnp.sin(angles)
    table = jnp.concatenate([cos_t, sin_t], axis=0).T
    turned_table = pltpu.roll(table, half, 1)
    low_lane = lax.broadcasted_iota(jnp.int32, (tokens, head_dim), 1) < half
    cos_q = jnp.where(low_lane, table, turned_table)
    sin_q = jnp.where(low_lane, -turned_table, table)

    gain = query_gain[...]
    per_part = wide // head_dim
    for part, load in enumerate(wq_loads):
        load.wait()
        projected = jnp.dot(
            states, wq[:, part * wide : (part + 1) * wide], preferred_element_type=jnp.float32
        )
        for local in range(per_part):
            value = projected[:, local * head_dim : (local + 1) * head_dim]
            mean_square = jnp.mean(value * value, axis=1, keepdims=True)
            value = value * lax.rsqrt(mean_square + 1e-06) * gain
            value = value * cos_q + pltpu.roll(value, half, 1) * sin_q
            at = (part * per_part + local) * tokens
            queries[at : at + tokens] = value.astype(jnp.bfloat16)

    group = min(4, heads_here)
    state = [None] * (heads_here // group)

    def attend(key_rows, value_rows, bias, keys_across=False):
        for head_id in range(heads_here // group):
            span = group * tokens
            query = queries[head_id * span : (head_id + 1) * span]
            if keys_across:
                scores = jnp.dot(query, key_rows, preferred_element_type=jnp.float32)
            else:
                scores = lax.dot_general(query, key_rows, NT, preferred_element_type=jnp.float32)
            scores = scores + bias
            top = jnp.max(scores, axis=1, keepdims=True)
            old = state[head_id]
            top = jnp.maximum(top, FLOOR if old is None else old[1])
            weights = jnp.exp2((scores - top) * scale)
            total = jnp.sum(weights, axis=1, keepdims=True)
            weights = weights.astype(jnp.bfloat16)
            if keys_across:
                summed = lax.dot_general(
                    weights, value_rows, NT, preferred_element_type=jnp.float32
                )
            else:
                summed = jnp.dot(weights, value_rows, preferred_element_type=jnp.float32)
            if old is not None:
                fade = jnp.exp2((old[1] - top) * scale)
                summed = summed + old[0] * fade
                total = total + old[2] * fade
            state[head_id] = (summed, top, total)

    def attend_step(step):
        start = slots if step == chips else 0
        stop = slots if step == 0 else 2 * slots
        count = stop - start
        lane = lax.broadcasted_iota(jnp.int32, (1, count), 1) + start
        here = chip_of(min(step, last)) * 2 + core
        other = chip_of(max(step - 1, 0)) * 2 + 1 - core
        source = jnp.where(lane < slots, here, other)
        position = source * slots + (lane & (slots - 1))
        bias = jnp.where(position < length[0], 0.0, LOW)
        span = pl.ds(start, count)
        at = mask_of(step)
        attend(held[at, 0, span], held[at, 1, span], bias)

    def attend_new():
        slab_passed_on.wait_recv()
        pick = lax.broadcasted_iota(jnp.int32, (2 * head_dim, 1), 0)
        kind, entry = pick >> log2_of(head_dim), pick & (head_dim - 1)
        source, deep = entry >> log2_of(depth), entry & (depth - 1)
        place = (source & 1) * chips + (source >> 1)
        joined = jnp.dot(
            one_hot(place * rows + kind * depth + deep, groups * rows),
            slab_in[...].reshape(groups * rows, tokens),
            preferred_element_type=jnp.float32,
        )
        key_raw = joined[:head_dim]
        value_new = joined[head_dim:].astype(jnp.bfloat16)
        gain_rows = jnp.broadcast_to(key_gain[...], (tokens, head_dim)).T
        mean_square = jnp.mean(key_raw * key_raw, axis=0, keepdims=True)
        normed = key_raw * lax.rsqrt(mean_square + 1e-06) * gain_rows
        upper, lower = normed[:half], normed[half:]
        key_new = jnp.concatenate(
            [upper * cos_t - lower * sin_t, lower * cos_t + upper * sin_t], axis=0
        ).astype(jnp.bfloat16)
        seen = lax.broadcasted_iota(jnp.int32, (group * tokens, tokens), 1)
        asks = lax.broadcasted_iota(jnp.int32, (group * tokens, tokens), 0) & (tokens - 1)
        attend(key_new, value_new, jnp.where(seen <= asks, 0.0, LOW), keys_across=True)

    for load in own:
        load.wait()
    attend_step(0)
    for step in range(1, chips):
        if step == 4:
            attend_new()
        arriving(step).wait()
        passes[step].start()
        if step == 3:
            own_slab.wait()
            for slab_copy in slabs:
                slab_copy.wait_recv()
            slab_passed_on.start()
        passes[step - 1].wait_recv()
        attend_step(step)
    for step in range(last):
        passes[step].wait_send()
    for slab_copy in slabs + [slab_passed_on]:
        slab_copy.wait_send()
    passes[last].wait_recv()
    attend_step(chips)

    for head_id in range(heads_here):
        summed, _, total = state[head_id // group]
        rows_of = slice(head_id % group * tokens, (head_id % group + 1) * tokens)
        out[:, head_id * head_dim : (head_id + 1) * head_dim] = (
            summed[rows_of] / total[rows_of]
        ).astype(jnp.bfloat16)

    for send in to_even + to_odd + [nearest] + near:
        send.wait_send()
    passes[last].wait_send()


def per_device(
    hidden,
    w_query,
    key_projection_weight,
    value_projection_weight,
    query_gain,
    key_gain,
    stored_cache_keys,
    stored_cache_values,
    cache_length,
    first_position,
):
    groups = lax.axis_size("ctx")
    tokens, width = hidden.shape
    head_dim = query_gain.shape[0]
    kv_heads = stored_cache_keys.shape[1] // head_dim
    slots = stored_cache_keys.shape[0]
    columns = key_projection_weight.shape[1]
    own_width = w_query.shape[1]
    rows = max(16, 2 * (columns // kv_heads))
    chips = groups // 2
    anywhere = pl.BlockSpec(memory_space=pltpu.HBM)
    vmem = pl.BlockSpec(memory_space=pltpu.VMEM)
    bf16 = jnp.bfloat16
    dma = pltpu.SemaphoreType.DMA
    return pl.pallas_call(
        functools.partial(kernel, groups, kv_heads),
        out_shape=pltpu.VMEM((tokens, own_width), bf16),
        in_specs=[anywhere] * 10,
        out_specs=vmem,
        scratch_shapes=[
            pltpu.VMEM((tokens, width), bf16),
            pltpu.VMEM((width, own_width), bf16),
            pltpu.VMEM((2 * columns, width), bf16),
            pltpu.VMEM((chips + 1, 2, 2 * slots, head_dim), bf16),
            pltpu.VMEM((kv_heads, rows, tokens), bf16),
            pltpu.VMEM((2, chips, rows, tokens), bf16),
            pltpu.VMEM((own_width // head_dim * tokens, head_dim), bf16),
            pltpu.VMEM((1, head_dim), jnp.float32),
            pltpu.VMEM((1, head_dim), jnp.float32),
            pltpu.SMEM((1,), jnp.int32),
            pltpu.SMEM((1,), jnp.int32),
            dma((9,)),
            dma((max(1, own_width // head_dim),)),
            dma((3,)),
            dma((chips,)),
            dma((chips,)),
            dma((chips,)),
            dma((chips,)),
            dma((chips,)),
            dma((chips,)),
            dma((chips,)),
            dma((chips,)),
            pltpu.SemaphoreType.REGULAR,
            pltpu.VMEM((2 * columns, tokens), jnp.float32),
        ],
        compiler_params=pltpu.CompilerParams(collective_id=0, has_side_effects=True),
    )(
        hidden,
        w_query,
        key_projection_weight.T,
        value_projection_weight.T,
        query_gain.reshape(1, head_dim),
        key_gain.reshape(1, head_dim),
        stored_cache_keys,
        stored_cache_values,
        cache_length,
        first_position,
    )


def solution(mesh):
    return jax.shard_map(
        per_device,
        mesh=mesh,
        in_specs=(
            P("req", None),
            P(None, "ctx"),
            P(None, "ctx"),
            P(None, "ctx"),
            P(),
            P(),
            P(("req", "ctx"), None),
            P(("req", "ctx"), None),
            P("req"),
            P("req"),
        ),
        out_specs=P("req", "ctx"),
        check_vma=False,
    )
```

```python
import functools
import math

import jax
import jax.numpy as jnp
from jax import lax
from jax.experimental import pallas as pl
from jax.experimental.pallas import tpu as pltpu
from jax.sharding import PartitionSpec as P

MESH = pl.DeviceIdType.MESH
LOW = -1e30
FLOOR = -1e29
NT = (((1,), (1,)), ((), ()))


def log2_of(value):
    bits = value.bit_length() - 1
    assert 1 << bits == value
    return bits


def flip(index, mask):
    out = index
    bit = 0
    while mask >> bit:
        if (mask >> bit) & 1:
            weight = 1 << bit
            out = out + weight * (1 - 2 * lax.rem(lax.div(index, weight), 2))
        bit += 1
    return out


def one_hot(target, columns):
    ids = lax.broadcasted_iota(jnp.int32, (target.shape[0], columns), 1)
    return jnp.where(ids == target, 1.0, 0.0).astype(jnp.bfloat16)


class Pair:
    def __init__(self, sources, target, send, recv, peer):
        self.copies = [
            pltpu.make_async_remote_copy(
                src_ref=source,
                dst_ref=target.at[kind],
                send_sem=send,
                recv_sem=recv,
                device_id={"ctx": peer},
                device_id_type=MESH,
            )
            for kind, source in enumerate(sources)
        ]
        self.target, self.send, self.recv = target, send, recv

    def start(self):
        for copy in self.copies:
            copy.start()

    def wait_send(self):
        pltpu.make_async_copy(self.target, self.target, self.send).wait()

    def wait_recv(self):
        pltpu.make_async_copy(self.target, self.target, self.recv).wait()


def kernel(
    groups,
    kv_heads,
    hidden_hbm,
    wq_hbm,
    wk_hbm,
    wv_hbm,
    query_gain_hbm,
    key_gain_hbm,
    keys_hbm,
    values_hbm,
    length_hbm,
    first_hbm,
    out,
    hid,
    wq,
    wkv,
    held,
    slab_out,
    slab_in,
    queries,
    query_gain,
    key_gain,
    length,
    first,
    load_sem,
    wq_sem,
    own_sem,
    send_sem,
    recv_sem,
    pass_sem,
    passed_sem,
    slab_send,
    slab_recv,
    slab_pass,
    slab_passed,
    late_sem,
):
    me = lax.axis_index("ctx")
    core, chip = lax.rem(me, 2), lax.div(me, 2)
    chips = groups // 2
    sharers = groups // kv_heads
    tokens, width = hid.shape
    head_dim = query_gain.shape[1]
    heads_here = wq.shape[1] // head_dim
    slots = keys_hbm.shape[0]
    columns = wkv.shape[0] // 2
    depth = columns // kv_heads
    rows = slab_out.shape[1]
    half = head_dim // 2
    scale = math.log2(math.e) / math.sqrt(head_dim)

    barrier = pltpu.get_barrier_semaphore()
    sibling = chip * 2 + (1 - core)
    last_plane = lax.div(chip, chips - 2)

    def greet(semaphore, peer):
        pl.semaphore_signal(semaphore, inc=1, device_id={"ctx": peer}, device_id_type=MESH)

    @pl.when(last_plane == 0)
    def _():
        for mask in reversed(range(2, chips)):
            greet(barrier, flip(chip, mask) * 2 + core)

    greet(barrier, flip(chip, 1) * 2 + core)
    greet(barrier, sibling)

    small_loads = [
        pltpu.make_async_copy(first_hbm, first, load_sem.at[5]),
        pltpu.make_async_copy(length_hbm, length, load_sem.at[6]),
        pltpu.make_async_copy(query_gain_hbm, query_gain, load_sem.at[7]),
        pltpu.make_async_copy(key_gain_hbm, key_gain, load_sem.at[8]),
    ]
    state_loads = [
        pltpu.make_async_copy(hidden_hbm, hid, load_sem.at[2]),
        pltpu.make_async_copy(wk_hbm, wkv.at[pl.ds(0, columns)], load_sem.at[3]),
        pltpu.make_async_copy(wv_hbm, wkv.at[pl.ds(columns, columns)], load_sem.at[4]),
    ]
    for load in state_loads:
        load.start()
    wide = min(2 * head_dim, wq.shape[1])
    wq_loads = []
    for part in range(wq.shape[1] // wide):
        cut = pl.ds(part * wide, wide)
        wq_loads.append(
            pltpu.make_async_copy(wq_hbm.at[:, cut], wq.at[:, cut], wq_sem.at[part])
        )

    def block_of(device):
        offset = pl.multiple_of((device // sharers) * head_dim, head_dim)
        columns_of = pl.ds(offset, head_dim)
        return [keys_hbm.at[:, columns_of], values_hbm.at[:, columns_of]]

    last = chips - 1
    middle = chips // 2
    low, high = lax.rem(lax.div(chip, 2), 2), lax.div(chip, middle)
    orders = [list(range(chips))] * 4
    if chips == 8:
        orders = [
            [0, 1, 6, 7, 2, 4, 3, 5],
            [0, 1, 2, 3, 4, 5, 6, 7],
            [0, 1, 4, 6, 7, 5, 2, 3],
            [0, 1, 2, 3, 6, 7, 4, 5],
        ]
    picks = [(1 - low) * (1 - high), low * (1 - high), (1 - low) * high, low * high]

    def by_place(values):
        return sum(pick * value for pick, value in zip(picks, values))

    def mask_of(step):
        masks = [order[step] for order in orders] if step < chips else [chips]
        return masks[0] if len(set(masks)) == 1 else by_place(masks)

    def chip_of(step):
        masks = [order[step] for order in orders]
        if len(set(masks)) == 1:
            return flip(chip, masks[0])
        return by_place([flip(chip, mask) for mask in masks])

    def sent(mask, to):
        peer = to * 2 + core
        return Pair(
            block_of(peer),
            held.at[mask, :, pl.ds(0, slots)],
            send_sem.at[0],
            recv_sem.at[mask],
            peer,
        )

    def bytes_of(place, semaphore):
        pltpu.make_async_copy(place, place, semaphore).wait()

    def arriving(step):
        mask = mask_of(step)
        place = held.at[mask, :, pl.ds(0, slots)]
        return pltpu.make_async_copy(place, place, recv_sem.at[mask])

    def forwarded(step):
        target = held.at[mask_of(step + 1), :, pl.ds(slots, slots)]
        if step == 0:
            return Pair(block_of(sibling), target, pass_sem.at[0], passed_sem.at[0], sibling)
        return pltpu.make_async_remote_copy(
            src_ref=held.at[mask_of(step), :, pl.ds(0, slots)],
            dst_ref=target,
            send_sem=pass_sem.at[0],
            recv_sem=passed_sem.at[step],
            device_id={"ctx": sibling},
            device_id_type=MESH,
        )

    to_even = [
        sent(mask + 2 * low, flip(chip, mask) - 2 * low)
        for mask in range(middle, chips)
        if not mask & 2
    ]
    to_odd = [
        sent(mask + 2 - 2 * low, flip(chip, mask) - 2 * low + 2)
        for mask in range(middle, chips)
        if not mask & 2
    ]
    nearest = sent(1, flip(chip, 1))
    near = [sent(mask, flip(chip, mask)) for mask in range(2, middle)]
    passes = {step: forwarded(step) for step in range(chips)}

    own = [
        pltpu.make_async_copy(block, held.at[0, kind, pl.ds(0, slots)], own_sem.at[kind])
        for kind, block in enumerate(block_of(me))
    ]
    for load in own:
        load.start()
    pl.semaphore_wait(barrier, chips - 2 + 2 * last_plane)

    @pl.when(last_plane == 1)
    def _():
        for mask in range(2, chips):
            greet(late_sem, flip(chip, mask) * 2 + core)

    for send in to_even[:1] + [nearest]:
        send.start()

    @pl.when(last_plane == 1)
    def _():
        for send in to_even[1:]:
            send.start()

    for load in state_loads:
        load.wait()
    for load in wq_loads + small_loads:
        load.start()
    states = hid[...]
    raw = lax.dot_general(
        wkv[...], states, NT, preferred_element_type=jnp.float32
    ).astype(jnp.bfloat16)
    row = lax.broadcasted_iota(jnp.int32, (kv_heads * rows, 1), 0)
    head, inner = row >> log2_of(rows), row & (rows - 1)
    which, deep = inner >> log2_of(depth), inner & (depth - 1)
    target = jnp.where(which < 2, which * columns + deep * kv_heads + head, -1)
    regrouped = jnp.dot(one_hot(target, 2 * columns), raw, preferred_element_type=jnp.float32)
    for head_id in range(kv_heads):
        slab_out[head_id] = regrouped[head_id * rows : (head_id + 1) * rows].astype(jnp.bfloat16)

    own_slab = pltpu.make_async_copy(
        slab_out.at[me // sharers], slab_in.at[core, chip], own_sem.at[2]
    )
    own_slab.start()

    def slab_to(mask, to):
        peer = to * 2 + core
        return pltpu.make_async_remote_copy(
            src_ref=slab_out.at[peer // sharers],
            dst_ref=slab_in.at[core, chip],
            send_sem=slab_send.at[0],
            recv_sem=slab_recv.at[0],
            device_id={"ctx": peer},
            device_id_type=MESH,
        )

    slabs = [slab_to(mask, flip(chip, mask)) for mask in range(1, chips)]
    slabs_even = [
        slab_to(mask + 2 * low, flip(chip, mask) - 2 * low)
        for mask in range(middle, chips)
        if not mask & 2
    ]
    slabs_odd = [
        slab_to(mask + 2 - 2 * low, flip(chip, mask) - 2 * low + 2)
        for mask in range(middle, chips)
        if not mask & 2
    ]

    for send in slabs[:1] + slabs_even:
        send.start()

    @pl.when(high == 0)
    def _():
        for send in slabs[1 : middle - 1] + near:
            send.start()

    @pl.when(last_plane == 0)
    def _():
        pl.semaphore_wait(late_sem, 2)

    for send in slabs_odd:
        send.start()

    @pl.when(high == 1)
    def _():
        for send in slabs[1 : middle - 1]:
            send.start()

    @pl.when(last_plane == 0)
    def _():
        for send in to_even[1:]:
            send.start()

    @pl.when(high == 1)
    def _():
        for send in near:
            send.start()

    for send in to_odd:
        send.start()

    passes[0].start()

    slab_passed_on = pltpu.make_async_remote_copy(
        src_ref=slab_in.at[core],
        dst_ref=slab_in.at[core],
        send_sem=slab_pass.at[0],
        recv_sem=slab_passed.at[0],
        device_id={"ctx": sibling},
        device_id_type=MESH,
    )
    for load in small_loads:
        load.wait()
    angle_row = lax.broadcasted_iota(jnp.int32, (half, tokens), 0).astype(jnp.float32)
    freq = jnp.exp(angle_row * (-2.0 * math.log(1000000.0) / head_dim))
    token_id = lax.broadcasted_iota(jnp.int32, (half, tokens), 1).astype(jnp.float32)
    angles = (first[0].astype(jnp.float32) + token_id) * freq
    cos_t, sin_t = jnp.cos(angles), jnp.sin(angles)
    table = jnp.concatenate([cos_t, sin_t], axis=0).T
    turned_table = pltpu.roll(table, half, 1)
    low_lane = lax.broadcasted_iota(jnp.int32, (tokens, head_dim), 1) < half
    cos_q = jnp.where(low_lane, table, turned_table)
    sin_q = jnp.where(low_lane, -turned_table, table)

    gain = query_gain[...]
    per_part = wide // head_dim
    for part, load in enumerate(wq_loads):
        load.wait()
        projected = jnp.dot(
            states, wq[:, part * wide : (part + 1) * wide], preferred_element_type=jnp.float32
        )
        for local in range(per_part):
            value = projected[:, local * head_dim : (local + 1) * head_dim]
            mean_square = jnp.mean(value * value, axis=1, keepdims=True)
            value = value * lax.rsqrt(mean_square + 1e-06) * gain
            value = value * cos_q + pltpu.roll(value, half, 1) * sin_q
            at = (part * per_part + local) * tokens
            queries[at : at + tokens] = value.astype(jnp.bfloat16)

    group = min(4, heads_here)
    state = [None] * (heads_here // group)

    def attend(key_rows, value_rows, bias, keys_across=False):
        for head_id in range(heads_here // group):
            span = group * tokens
            query = queries[head_id * span : (head_id + 1) * span]
            if keys_across:
                scores = jnp.dot(query, key_rows, preferred_element_type=jnp.float32)
            else:
                scores = lax.dot_general(query, key_rows, NT, preferred_element_type=jnp.float32)
            scores = scores + bias
            top = jnp.max(scores, axis=1, keepdims=True)
            old = state[head_id]
            top = jnp.maximum(top, FLOOR if old is None else old[1])
            weights = jnp.exp2((scores - top) * scale)
            total = jnp.sum(weights, axis=1, keepdims=True)
            weights = weights.astype(jnp.bfloat16)
            if keys_across:
                summed = lax.dot_general(
                    weights, value_rows, NT, preferred_element_type=jnp.float32
                )
            else:
                summed = jnp.dot(weights, value_rows, preferred_element_type=jnp.float32)
            if old is not None:
                fade = jnp.exp2((old[1] - top) * scale)
                summed = summed + old[0] * fade
                total = total + old[2] * fade
            state[head_id] = (summed, top, total)

    def attend_step(step):
        start = slots if step == chips else 0
        stop = slots if step == 0 else 2 * slots
        count = stop - start
        lane = lax.broadcasted_iota(jnp.int32, (1, count), 1) + start
        here = chip_of(min(step, last)) * 2 + core
        other = chip_of(max(step - 1, 0)) * 2 + 1 - core
        source = jnp.where(lane < slots, here, other)
        position = source * slots + (lane & (slots - 1))
        bias = jnp.where(position < length[0], 0.0, LOW)
        span = pl.ds(start, count)
        at = mask_of(step)
        attend(held[at, 0, span], held[at, 1, span], bias)

    def attend_new():
        slab_passed_on.wait_recv()
        pick = lax.broadcasted_iota(jnp.int32, (2 * head_dim, 1), 0)
        kind, entry = pick >> log2_of(head_dim), pick & (head_dim - 1)
        source, deep = entry >> log2_of(depth), entry & (depth - 1)
        place = (source & 1) * chips + (source >> 1)
        joined = jnp.dot(
            one_hot(place * rows + kind * depth + deep, groups * rows),
            slab_in[...].reshape(groups * rows, tokens),
            preferred_element_type=jnp.float32,
        )
        key_raw = joined[:head_dim]
        value_new = joined[head_dim:].astype(jnp.bfloat16)
        gain_rows = jnp.broadcast_to(key_gain[...], (tokens, head_dim)).T
        mean_square = jnp.mean(key_raw * key_raw, axis=0, keepdims=True)
        normed = key_raw * lax.rsqrt(mean_square + 1e-06) * gain_rows
        upper, lower = normed[:half], normed[half:]
        key_new = jnp.concatenate(
            [upper * cos_t - lower * sin_t, lower * cos_t + upper * sin_t], axis=0
        ).astype(jnp.bfloat16)
        seen = lax.broadcasted_iota(jnp.int32, (group * tokens, tokens), 1)
        asks = lax.broadcasted_iota(jnp.int32, (group * tokens, tokens), 0) & (tokens - 1)
        attend(key_new, value_new, jnp.where(seen <= asks, 0.0, LOW), keys_across=True)

    for load in own:
        load.wait()
    attend_step(0)
    for step in range(1, chips):
        arriving(step).wait()
        passes[step].start()
        if step == 3:
            own_slab.wait()
            bytes_of(slab_in.at[core, pl.ds(0, last)], slab_recv.at[0])
            slab_passed_on.start()
        if step == 4:
            attend_new()
        passes[step - 1].wait_recv()
        attend_step(step)
    passes[last].wait_recv()
    attend_step(chips)

    for head_id in range(heads_here):
        summed, _, total = state[head_id // group]
        rows_of = slice(head_id % group * tokens, (head_id % group + 1) * tokens)
        out[:, head_id * head_dim : (head_id + 1) * head_dim] = (
            summed[rows_of] / total[rows_of]
        ).astype(jnp.bfloat16)

    bytes_of(held.at[pl.ds(0, last), :, pl.ds(0, slots)], send_sem.at[0])
    bytes_of(held.at[pl.ds(0, chips), :, pl.ds(0, slots)], pass_sem.at[0])
    bytes_of(slab_in.at[core, pl.ds(0, last)], slab_send.at[0])
    slab_passed_on.wait_send()


def per_device(
    hidden,
    w_query,
    key_projection_weight,
    value_projection_weight,
    query_gain,
    key_gain,
    stored_cache_keys,
    stored_cache_values,
    cache_length,
    first_position,
):
    groups = lax.axis_size("ctx")
    tokens, width = hidden.shape
    head_dim = query_gain.shape[0]
    kv_heads = stored_cache_keys.shape[1] // head_dim
    slots = stored_cache_keys.shape[0]
    columns = key_projection_weight.shape[1]
    own_width = w_query.shape[1]
    rows = max(16, 2 * (columns // kv_heads))
    chips = groups // 2
    anywhere = pl.BlockSpec(memory_space=pltpu.HBM)
    vmem = pl.BlockSpec(memory_space=pltpu.VMEM)
    bf16 = jnp.bfloat16
    dma = pltpu.SemaphoreType.DMA
    return pl.pallas_call(
        functools.partial(kernel, groups, kv_heads),
        out_shape=pltpu.VMEM((tokens, own_width), bf16),
        in_specs=[anywhere] * 10,
        out_specs=vmem,
        scratch_shapes=[
            pltpu.VMEM((tokens, width), bf16),
            pltpu.VMEM((width, own_width), bf16),
            pltpu.VMEM((2 * columns, width), bf16),
            pltpu.VMEM((chips + 1, 2, 2 * slots, head_dim), bf16),
            pltpu.VMEM((kv_heads, rows, tokens), bf16),
            pltpu.VMEM((2, chips, rows, tokens), bf16),
            pltpu.VMEM((own_width // head_dim * tokens, head_dim), bf16),
            pltpu.VMEM((1, head_dim), jnp.float32),
            pltpu.VMEM((1, head_dim), jnp.float32),
            pltpu.SMEM((1,), jnp.int32),
            pltpu.SMEM((1,), jnp.int32),
            dma((9,)),
            dma((max(1, own_width // head_dim),)),
            dma((3,)),
            dma((chips,)),
            dma((chips,)),
            dma((chips,)),
            dma((chips,)),
            dma((chips,)),
            dma((chips,)),
            dma((chips,)),
            dma((chips,)),
            pltpu.SemaphoreType.REGULAR,
        ],
        compiler_params=pltpu.CompilerParams(collective_id=0, has_side_effects=True),
    )(
        hidden,
        w_query,
        key_projection_weight.T,
        value_projection_weight.T,
        query_gain.reshape(1, head_dim),
        key_gain.reshape(1, head_dim),
        stored_cache_keys,
        stored_cache_values,
        cache_length,
        first_position,
    )


def solution(mesh):
    return jax.shard_map(
        per_device,
        mesh=mesh,
        in_specs=(
            P("req", None),
            P(None, "ctx"),
            P(None, "ctx"),
            P(None, "ctx"),
            P(),
            P(),
            P(("req", "ctx"), None),
            P(("req", "ctx"), None),
            P("req"),
            P("req"),
        ),
        out_specs=P("req", "ctx"),
        check_vma=False,
    )
```

```python
import functools
import math

import jax
import jax.numpy as jnp
from jax import lax
from jax.experimental import pallas as pl
from jax.experimental.pallas import tpu as pltpu
from jax.sharding import PartitionSpec as P

MESH = pl.DeviceIdType.MESH
LOW = -1e30
FLOOR = -1e29
NT = (((1,), (1,)), ((), ()))


def log2_of(value):
    bits = value.bit_length() - 1
    assert 1 << bits == value
    return bits


def flip(index, mask):
    out = index
    bit = 0
    while mask >> bit:
        if (mask >> bit) & 1:
            weight = 1 << bit
            out = out + weight * (1 - 2 * lax.rem(lax.div(index, weight), 2))
        bit += 1
    return out


def one_hot(target, columns):
    ids = lax.broadcasted_iota(jnp.int32, (target.shape[0], columns), 1)
    return jnp.where(ids == target, 1.0, 0.0).astype(jnp.bfloat16)


class Pair:
    def __init__(self, sources, target, send, recv, peer):
        self.copies = [
            pltpu.make_async_remote_copy(
                src_ref=source,
                dst_ref=target.at[kind],
                send_sem=send,
                recv_sem=recv,
                device_id={"ctx": peer},
                device_id_type=MESH,
            )
            for kind, source in enumerate(sources)
        ]
        self.target, self.send, self.recv = target, send, recv

    def start(self):
        for copy in self.copies:
            copy.start()

    def wait_send(self):
        pltpu.make_async_copy(self.target, self.target, self.send).wait()

    def wait_recv(self):
        pltpu.make_async_copy(self.target, self.target, self.recv).wait()


def kernel(
    groups,
    kv_heads,
    hidden_hbm,
    wq_hbm,
    wk_hbm,
    wv_hbm,
    query_gain_hbm,
    key_gain_hbm,
    keys_hbm,
    values_hbm,
    length_hbm,
    first_hbm,
    out,
    hid,
    wq,
    wkv,
    held,
    slab_out,
    slab_in,
    queries,
    query_gain,
    key_gain,
    length,
    first,
    load_sem,
    wq_sem,
    own_sem,
    send_sem,
    recv_sem,
    pass_sem,
    passed_sem,
    slab_send,
    slab_recv,
    slab_pass,
    slab_passed,
    stage,
    late_sem,
    raw_rows,
):
    me = lax.axis_index("ctx")
    core, chip = lax.rem(me, 2), lax.div(me, 2)
    chips = groups // 2
    sharers = groups // kv_heads
    tokens, width = hid.shape
    head_dim = query_gain.shape[1]
    heads_here = wq.shape[1] // head_dim
    slots = keys_hbm.shape[0]
    columns = wkv.shape[0] // 2
    depth = columns // kv_heads
    rows = slab_out.shape[1]
    half = head_dim // 2
    scale = math.log2(math.e) / math.sqrt(head_dim)

    barrier = pltpu.get_barrier_semaphore()
    sibling = chip * 2 + (1 - core)
    last_plane = lax.div(chip, chips - 2)

    def greet(semaphore, peer):
        pl.semaphore_signal(semaphore, inc=1, device_id={"ctx": peer}, device_id_type=MESH)

    @pl.when(last_plane == 0)
    def _():
        for mask in reversed(range(2, chips)):
            greet(barrier, flip(chip, mask) * 2 + core)

    greet(barrier, flip(chip, 1) * 2 + core)
    greet(barrier, sibling)

    small_loads = [
        pltpu.make_async_copy(first_hbm, first, load_sem.at[5]),
        pltpu.make_async_copy(length_hbm, length, load_sem.at[6]),
        pltpu.make_async_copy(query_gain_hbm, query_gain, load_sem.at[7]),
        pltpu.make_async_copy(key_gain_hbm, key_gain, load_sem.at[8]),
    ]
    state_loads = [
        pltpu.make_async_copy(hidden_hbm, hid, load_sem.at[2]),
        pltpu.make_async_copy(wk_hbm, wkv.at[pl.ds(0, columns)], load_sem.at[3]),
        pltpu.make_async_copy(wv_hbm, wkv.at[pl.ds(columns, columns)], load_sem.at[4]),
    ]
    stage_loads = [
        pltpu.make_async_copy(keys_hbm, stage.at[0], load_sem.at[0]),
        pltpu.make_async_copy(values_hbm, stage.at[1], load_sem.at[1]),
    ]
    for load in state_loads + stage_loads:
        load.start()
    wide = min(2 * head_dim, wq.shape[1])
    wq_loads = []
    for part in range(wq.shape[1] // wide):
        cut = pl.ds(part * wide, wide)
        wq_loads.append(
            pltpu.make_async_copy(wq_hbm.at[:, cut], wq.at[:, cut], wq_sem.at[part])
        )

    def block_of(device):
        offset = pl.multiple_of((device // sharers) * head_dim, head_dim)
        columns_of = pl.ds(offset, head_dim)
        return [keys_hbm.at[:, columns_of], values_hbm.at[:, columns_of]]

    last = chips - 1
    middle = chips // 2
    low, high = lax.rem(lax.div(chip, 2), 2), lax.div(chip, middle)
    orders = [list(range(chips))] * 4
    if chips == 8:
        orders = [
            [0, 1, 6, 7, 4, 5, 2, 3],
            [0, 1, 2, 3, 4, 5, 6, 7],
            [0, 1, 4, 6, 7, 2, 5, 3],
            [0, 1, 2, 3, 6, 7, 4, 5],
        ]
    picks = [(1 - low) * (1 - high), low * (1 - high), (1 - low) * high, low * high]

    def by_place(values):
        return sum(pick * value for pick, value in zip(picks, values))

    def mask_of(step):
        masks = [order[step] for order in orders] if step < chips else [chips]
        return masks[0] if len(set(masks)) == 1 else by_place(masks)

    def chip_of(step):
        masks = [order[step] for order in orders]
        if len(set(masks)) == 1:
            return flip(chip, masks[0])
        return by_place([flip(chip, mask) for mask in masks])

    def sent(mask, to):
        peer = to * 2 + core
        return Pair(
            block_of(peer),
            held.at[mask, :, pl.ds(0, slots)],
            send_sem.at[0],
            recv_sem.at[mask],
            peer,
        )

    def bytes_of(place, semaphore):
        pltpu.make_async_copy(place, place, semaphore).wait()

    def staged(mask, to):
        peer = to * 2 + core
        offset = pl.multiple_of((peer // sharers) * head_dim, head_dim)
        return pltpu.make_async_remote_copy(
            src_ref=stage.at[:, :, pl.ds(offset, head_dim)],
            dst_ref=held.at[mask, :, pl.ds(0, slots)],
            send_sem=send_sem.at[0],
            recv_sem=recv_sem.at[mask],
            device_id={"ctx": peer},
            device_id_type=MESH,
        )

    def arriving(step):
        mask = mask_of(step)
        place = held.at[mask, :, pl.ds(0, slots)]
        return pltpu.make_async_copy(place, place, recv_sem.at[mask])

    def forwarded(step):
        target = held.at[mask_of(step + 1), :, pl.ds(slots, slots)]
        if step == 0:
            return Pair(block_of(sibling), target, pass_sem.at[0], passed_sem.at[0], sibling)
        return pltpu.make_async_remote_copy(
            src_ref=held.at[mask_of(step), :, pl.ds(0, slots)],
            dst_ref=target,
            send_sem=pass_sem.at[0],
            recv_sem=passed_sem.at[step],
            device_id={"ctx": sibling},
            device_id_type=MESH,
        )

    to_even = [
        sent(mask + 2 * low, flip(chip, mask) - 2 * low)
        for mask in range(middle, chips)
        if not mask & 2
    ]
    to_odd = [
        staged(mask + 2 - 2 * low, flip(chip, mask) - 2 * low + 2)
        for mask in range(middle, chips)
        if not mask & 2
    ]
    nearest = sent(1, flip(chip, 1))
    near = [staged(mask, flip(chip, mask)) for mask in range(2, middle)]
    passes = {step: forwarded(step) for step in range(chips)}

    own = [
        pltpu.make_async_copy(block, held.at[0, kind, pl.ds(0, slots)], own_sem.at[kind])
        for kind, block in enumerate(block_of(me))
    ]
    for load in own:
        load.start()
    pl.semaphore_wait(barrier, chips - 2 + 2 * last_plane)

    @pl.when(last_plane == 1)
    def _():
        for mask in range(2, chips):
            greet(late_sem, flip(chip, mask) * 2 + core)

    for send in to_even[:1] + [nearest]:
        send.start()

    @pl.when(last_plane == 1)
    def _():
        for send in to_even[1:]:
            send.start()

    for load in state_loads:
        load.wait()
    for load in wq_loads + small_loads:
        load.start()
    states = hid[...]
    raw = lax.dot_general(
        wkv[...], states, NT, preferred_element_type=jnp.float32
    ).astype(jnp.bfloat16)
    raw_rows[...] = raw.astype(jnp.float32)
    for head_id in range(kv_heads):
        slab = raw_rows[pl.ds(head_id, 2 * depth, stride=kv_heads)]
        if 2 * depth < rows:
            slab = jnp.concatenate(
                [slab, jnp.zeros((rows - 2 * depth, tokens), jnp.float32)], axis=0
            )
        slab_out[head_id] = slab.astype(jnp.bfloat16)

    own_slab = pltpu.make_async_copy(
        slab_out.at[me // sharers], slab_in.at[core, chip], own_sem.at[2]
    )
    own_slab.start()

    def slab_to(mask, to):
        peer = to * 2 + core
        return pltpu.make_async_remote_copy(
            src_ref=slab_out.at[peer // sharers],
            dst_ref=slab_in.at[core, chip],
            send_sem=slab_send.at[0],
            recv_sem=slab_recv.at[0],
            device_id={"ctx": peer},
            device_id_type=MESH,
        )

    slabs = [slab_to(mask, flip(chip, mask)) for mask in range(1, chips)]
    slabs_even = [
        slab_to(mask + 2 * low, flip(chip, mask) - 2 * low)
        for mask in range(middle, chips)
        if not mask & 2
    ]
    slabs_odd = [
        slab_to(mask + 2 - 2 * low, flip(chip, mask) - 2 * low + 2)
        for mask in range(middle, chips)
        if not mask & 2
    ]

    for send in slabs[:1] + slabs_even:
        send.start()
    for load in stage_loads:
        load.wait()

    @pl.when(high == 0)
    def _():
        for send in slabs[1 : middle - 1] + near:
            send.start()

    @pl.when(last_plane == 0)
    def _():
        pl.semaphore_wait(late_sem, 2)

    for send in slabs_odd:
        send.start()

    @pl.when(high == 1)
    def _():
        for send in slabs[1 : middle - 1]:
            send.start()

    @pl.when(last_plane == 0)
    def _():
        for send in to_even[1:]:
            send.start()

    @pl.when(high == 1)
    def _():
        for send in near:
            send.start()

    for send in to_odd:
        send.start()

    passes[0].start()

    slab_passed_on = pltpu.make_async_remote_copy(
        src_ref=slab_in.at[core],
        dst_ref=slab_in.at[core],
        send_sem=slab_pass.at[0],
        recv_sem=slab_passed.at[0],
        device_id={"ctx": sibling},
        device_id_type=MESH,
    )
    for load in small_loads:
        load.wait()
    angle_row = lax.broadcasted_iota(jnp.int32, (half, tokens), 0).astype(jnp.float32)
    freq = jnp.exp(angle_row * (-2.0 * math.log(1000000.0) / head_dim))
    token_id = lax.broadcasted_iota(jnp.int32, (half, tokens), 1).astype(jnp.float32)
    angles = (first[0].astype(jnp.float32) + token_id) * freq
    cos_t, sin_t = jnp.cos(angles), jnp.sin(angles)
    table = jnp.concatenate([cos_t, sin_t], axis=0).T
    turned_table = pltpu.roll(table, half, 1)
    low_lane = lax.broadcasted_iota(jnp.int32, (tokens, head_dim), 1) < half
    cos_q = jnp.where(low_lane, table, turned_table)
    sin_q = jnp.where(low_lane, -turned_table, table)

    gain = query_gain[...]
    per_part = wide // head_dim
    for part, load in enumerate(wq_loads):
        load.wait()
        projected = jnp.dot(
            states, wq[:, part * wide : (part + 1) * wide], preferred_element_type=jnp.float32
        )
        for local in range(per_part):
            value = projected[:, local * head_dim : (local + 1) * head_dim]
            mean_square = jnp.mean(value * value, axis=1, keepdims=True)
            value = value * lax.rsqrt(mean_square + 1e-06) * gain
            value = value * cos_q + pltpu.roll(value, half, 1) * sin_q
            at = (part * per_part + local) * tokens
            queries[at : at + tokens] = value.astype(jnp.bfloat16)

    group = min(4, heads_here)
    state = [None] * (heads_here // group)

    def attend(key_rows, value_rows, bias, keys_across=False):
        for head_id in range(heads_here // group):
            span = group * tokens
            query = queries[head_id * span : (head_id + 1) * span]
            if keys_across:
                scores = jnp.dot(query, key_rows, preferred_element_type=jnp.float32)
            else:
                scores = lax.dot_general(query, key_rows, NT, preferred_element_type=jnp.float32)
            scores = scores + bias
            top = jnp.max(scores, axis=1, keepdims=True)
            old = state[head_id]
            top = jnp.maximum(top, FLOOR if old is None else old[1])
            weights = jnp.exp2((scores - top) * scale)
            total = jnp.sum(weights, axis=1, keepdims=True)
            weights = weights.astype(jnp.bfloat16)
            if keys_across:
                summed = lax.dot_general(
                    weights, value_rows, NT, preferred_element_type=jnp.float32
                )
            else:
                summed = jnp.dot(weights, value_rows, preferred_element_type=jnp.float32)
            if old is not None:
                fade = jnp.exp2((old[1] - top) * scale)
                summed = summed + old[0] * fade
                total = total + old[2] * fade
            state[head_id] = (summed, top, total)

    def attend_step(step):
        start = slots if step == chips else 0
        stop = slots if step == 0 else 2 * slots
        count = stop - start
        lane = lax.broadcasted_iota(jnp.int32, (1, count), 1) + start
        here = chip_of(min(step, last)) * 2 + core
        other = chip_of(max(step - 1, 0)) * 2 + 1 - core
        source = jnp.where(lane < slots, here, other)
        position = source * slots + (lane & (slots - 1))
        bias = jnp.where(position < length[0], 0.0, LOW)
        span = pl.ds(start, count)
        at = mask_of(step)
        attend(held[at, 0, span], held[at, 1, span], bias)

    def attend_new():
        slab_passed_on.wait_recv()
        pick = lax.broadcasted_iota(jnp.int32, (2 * head_dim, 1), 0)
        kind, entry = pick >> log2_of(head_dim), pick & (head_dim - 1)
        source, deep = entry >> log2_of(depth), entry & (depth - 1)
        place = (source & 1) * chips + (source >> 1)
        joined = jnp.dot(
            one_hot(place * rows + kind * depth + deep, groups * rows),
            slab_in[...].reshape(groups * rows, tokens),
            preferred_element_type=jnp.float32,
        )
        key_raw = joined[:head_dim]
        value_new = joined[head_dim:].astype(jnp.bfloat16)
        gain_rows = jnp.broadcast_to(key_gain[...], (tokens, head_dim)).T
        mean_square = jnp.mean(key_raw * key_raw, axis=0, keepdims=True)
        normed = key_raw * lax.rsqrt(mean_square + 1e-06) * gain_rows
        upper, lower = normed[:half], normed[half:]
        key_new = jnp.concatenate(
            [upper * cos_t - lower * sin_t, lower * cos_t + upper * sin_t], axis=0
        ).astype(jnp.bfloat16)
        seen = lax.broadcasted_iota(jnp.int32, (group * tokens, tokens), 1)
        asks = lax.broadcasted_iota(jnp.int32, (group * tokens, tokens), 0) & (tokens - 1)
        attend(key_new, value_new, jnp.where(seen <= asks, 0.0, LOW), keys_across=True)

    for load in own:
        load.wait()
    attend_step(0)
    for step in range(1, chips):
        if step == 4:
            attend_new()
        arriving(step).wait()
        passes[step].start()
        if step == 3:
            own_slab.wait()
            bytes_of(slab_in.at[core, pl.ds(0, last)], slab_recv.at[0])
            slab_passed_on.start()
        passes[step - 1].wait_recv()
        attend_step(step)
    passes[last].wait_recv()
    attend_step(chips)

    for head_id in range(heads_here):
        summed, _, total = state[head_id // group]
        rows_of = slice(head_id % group * tokens, (head_id % group + 1) * tokens)
        out[:, head_id * head_dim : (head_id + 1) * head_dim] = (
            summed[rows_of] / total[rows_of]
        ).astype(jnp.bfloat16)

    bytes_of(held.at[pl.ds(0, last), :, pl.ds(0, slots)], send_sem.at[0])
    bytes_of(held.at[pl.ds(0, chips), :, pl.ds(0, slots)], pass_sem.at[0])
    bytes_of(slab_in.at[core, pl.ds(0, last)], slab_send.at[0])
    slab_passed_on.wait_send()


def per_device(
    hidden,
    w_query,
    key_projection_weight,
    value_projection_weight,
    query_gain,
    key_gain,
    stored_cache_keys,
    stored_cache_values,
    cache_length,
    first_position,
):
    groups = lax.axis_size("ctx")
    tokens, width = hidden.shape
    head_dim = query_gain.shape[0]
    kv_heads = stored_cache_keys.shape[1] // head_dim
    slots = stored_cache_keys.shape[0]
    columns = key_projection_weight.shape[1]
    own_width = w_query.shape[1]
    rows = max(16, 2 * (columns // kv_heads))
    chips = groups // 2
    anywhere = pl.BlockSpec(memory_space=pltpu.HBM)
    vmem = pl.BlockSpec(memory_space=pltpu.VMEM)
    bf16 = jnp.bfloat16
    dma = pltpu.SemaphoreType.DMA
    return pl.pallas_call(
        functools.partial(kernel, groups, kv_heads),
        out_shape=pltpu.VMEM((tokens, own_width), bf16),
        in_specs=[anywhere] * 10,
        out_specs=vmem,
        scratch_shapes=[
            pltpu.VMEM((tokens, width), bf16),
            pltpu.VMEM((width, own_width), bf16),
            pltpu.VMEM((2 * columns, width), bf16),
            pltpu.VMEM((chips + 1, 2, 2 * slots, head_dim), bf16),
            pltpu.VMEM((kv_heads, rows, tokens), bf16),
            pltpu.VMEM((2, chips, rows, tokens), bf16),
            pltpu.VMEM((own_width // head_dim * tokens, head_dim), bf16),
            pltpu.VMEM((1, head_dim), jnp.float32),
            pltpu.VMEM((1, head_dim), jnp.float32),
            pltpu.SMEM((1,), jnp.int32),
            pltpu.SMEM((1,), jnp.int32),
            dma((9,)),
            dma((max(1, own_width // head_dim),)),
            dma((3,)),
            dma((chips,)),
            dma((chips,)),
            dma((chips,)),
            dma((chips,)),
            dma((chips,)),
            dma((chips,)),
            dma((chips,)),
            dma((chips,)),
            pltpu.VMEM((2, slots, kv_heads * head_dim), bf16),
            pltpu.SemaphoreType.REGULAR,
            pltpu.VMEM((2 * columns, tokens), jnp.float32),
        ],
        compiler_params=pltpu.CompilerParams(collective_id=0, has_side_effects=True),
    )(
        hidden,
        w_query,
        key_projection_weight.T,
        value_projection_weight.T,
        query_gain.reshape(1, head_dim),
        key_gain.reshape(1, head_dim),
        stored_cache_keys,
        stored_cache_values,
        cache_length,
        first_position,
    )


def solution(mesh):
    return jax.shard_map(
        per_device,
        mesh=mesh,
        in_specs=(
            P("req", None),
            P(None, "ctx"),
            P(None, "ctx"),
            P(None, "ctx"),
            P(),
            P(),
            P(("req", "ctx"), None),
            P(("req", "ctx"), None),
            P("req"),
            P("req"),
        ),
        out_specs=P("req", "ctx"),
        check_vma=False,
    )
```
